32 devices in a mesh: seq: 8 (over z, y), head: 4 (over x, core).
Axes of the slice: x: 2, y: 2, z: 4, core: 2. Of those that a mesh axis runs over, the one named last changes fastest.
Arguments:
- queries: bfloat16 [8192, 32, 128], P('seq', 'head'), may hold values from -150 to 150
- keyvals: bfloat16 [8192, 4, 128], P('seq', 'head'), may hold values from -6.5 to 6.5
- selected: int32 [128, 16], P('seq'), may hold values from 0 to 127, as said below
- d_out: bfloat16 [8192, 32, 128], P('seq', 'head'), may hold values from -40 to 40
Outputs:
- grad_queries: bfloat16 [8192, 32, 128], P('seq', 'head')
- grad_kv: bfloat16 [8192, 4, 128], P('seq', 'head')
The draws below stay inside these ranges and needn't reach their ends.
Inputs may be any that keep to these rules, and one draw needn't show every extreme that they name: `selected`: tiles form shards of 16 in order, as do the query blocks. Block b names tile 0 in slot 0, tile b in slot 1 and tile max(b - 1, 0) in slot 2, and no tile above b; tiles may repeat in a row. So slot 0 names a tile of shard 0, and slot 2 of the first block of a shard d >= 1 names a tile of shard d - 1. In blocks of shard d >= 1, slots 3 to 8 name tiles of lower shards; in blocks of shard 0 they name tiles of shard 0; slots 6 + 3 to 15 of every block name tiles of the block's own shard. For every shard d >= 1 and every lower shard e, the blocks of d together name, over all their slots, exactly 3 distinct tiles of e.
All inputs are finite; a program needn't handle non-finite values.
Results may differ from the reference program's by a relative error of at most 0.005.
Values may be sent and summed in bfloat16 or wider, within the bound.
No kernel may reach another device: no remote copies, remote signals or barrier semaphores. Data moves between devices by JAX's collectives and lax.ppermute only.
A program may use at most 128 MiB of HBM per device.

```python
import jax
import jax.numpy as jnp
from jax import lax

DH = 128
TILE = 64
SEL = 16
CAP = 3
REMOTE = 6
BLK_DEV = 16
BLOCKS = 128
SEQ_LEN = 8192
HEADS = 32
GROUP = 16
KV_HEADS = 2


def keyval_base(key):
    normal_draw = jax.random.normal(jax.random.fold_in(key, 7), (SEQ_LEN, 2 * KV_HEADS, DH), jnp.float32)
    normal_draw = jnp.clip(normal_draw, -6.0, 6.0)
    return normal_draw


def draw_keyvals(key, part):
    return keyval_base(key).astype(jnp.bfloat16)


def draw_queries(key, part):
    normal_draw = jax.random.normal(jax.random.fold_in(key, 9), (SEQ_LEN, HEADS, DH), jnp.float32)
    normal_draw = jnp.clip(normal_draw, -6.0, 6.0)
    return normal_draw.astype(jnp.bfloat16)


def draw_selected(key, part):
    shards = BLOCKS // BLK_DEV
    local_ids = jnp.arange(BLK_DEV, dtype=jnp.int32)
    ranks = jax.random.randint(jax.random.fold_in(key, 21), (shards, shards, BLK_DEV), 0, 1 << 16)
    ranks = ranks * BLK_DEV + local_ids[None, None, :]
    req_shard = jnp.arange(shards, dtype=jnp.int32)[:, None, None]
    own_shard = jnp.arange(shards, dtype=jnp.int32)[None, :, None]
    ranks = jnp.where((own_shard == 0) & (local_ids[None, None, :] == 0), -2, ranks)
    ranks = jnp.where((own_shard == req_shard - 1) & (local_ids[None, None, :] == BLK_DEV - 1), -1, ranks)
    menu_tiles = jnp.argsort(ranks, axis=-1)[..., :CAP].astype(jnp.int32)
    block_ids = jnp.arange(BLOCKS, dtype=jnp.int32)
    shard_ids = block_ids // BLK_DEV
    row_ids = block_ids % BLK_DEV
    rotation = jax.random.randint(jax.random.fold_in(key, 22), (shards,), 0, 1 << 16).astype(jnp.int32)
    menu_size = jnp.maximum(shard_ids * CAP, 1)
    turn_ids = jnp.arange(REMOTE, dtype=jnp.int32)
    cycle_pos = (row_ids[:, None] * REMOTE + turn_ids[None, :] + rotation[shard_ids][:, None]) % menu_size[:, None]
    src_shard = cycle_pos // CAP
    cell_ids = cycle_pos % CAP
    far_tiles = src_shard * BLK_DEV + menu_tiles[shard_ids[:, None], src_shard, cell_ids]
    first_tile = shard_ids * BLK_DEV
    near_tiles = jax.random.randint(jax.random.fold_in(key, 23), (BLOCKS, SEL - 3), first_tile[:, None], block_ids[:, None] + 1).astype(jnp.int32)
    remote = jnp.where((shard_ids > 0)[:, None], far_tiles, near_tiles[:, :REMOTE])
    rest_tiles = near_tiles[:, REMOTE:]
    fixed_tiles = jnp.stack([jnp.zeros_like(block_ids), block_ids, jnp.maximum(block_ids - 1, 0)], axis=1)
    return jnp.concatenate([fixed_tiles, remote, rest_tiles], axis=1).astype(jnp.int32)


def steps_of(stream_key, dims, cuts, smallest, largest):
    factor_of = 1.0
    for position, blocks in cuts:
        steps = jax.random.uniform(jax.random.fold_in(jax.random.fold_in(stream_key, 6), position), (blocks,), jnp.float32, smallest / len(cuts), largest / len(cuts))
        factor_of = factor_of * jnp.repeat(jnp.exp(steps), dims[position] // blocks).reshape((-1,) + (1,) * (len(dims) - 1 - position))
    return factor_of


def bell_draw(key, dims, deviation, limit, cuts=(), kind=jnp.bfloat16):
    drawn = deviation * jax.random.normal(key, dims, jnp.float32)
    if cuts:
        drawn = drawn * steps_of(key, dims, cuts, -0.22, 0.18)
    return jnp.clip(drawn, -limit, limit).astype(kind)


def setup_inputs(seed: int = 0) -> dict:
    seeds = jax.random.split(jax.random.key(seed), 5)
    return {
        "queries": draw_queries(jax.random.fold_in(seeds[4], 71), 0),
        "keyvals": draw_keyvals(jax.random.fold_in(seeds[4], 71), 0),
        "selected": draw_selected(jax.random.fold_in(seeds[4], 71), 0),
        "d_out": bell_draw(seeds[3], (SEQ_LEN, HEADS, DH), 8.0, 40.0, ((0, 8), (1, 4))),
    }


def live_slots(selected):
    slot_ids = jnp.arange(SEL, dtype=jnp.int32)
    earlier = slot_ids[None, :] < slot_ids[:, None]
    repeats = selected[:, :, None] == selected[:, None, :]
    return jnp.logical_not(jnp.any(repeats & earlier[None, :, :], axis=2))


def attend_tiles(query_blk, dout_blk, key_sel, value_sel, live_mask, block_ids, sel_ids):
    inv_root = DH ** -0.5
    query_pos = block_ids[:, None] * TILE + jnp.arange(TILE, dtype=jnp.int32)[None, :]
    key_pos = (sel_ids[:, :, None] * TILE + jnp.arange(TILE, dtype=jnp.int32)[None, None, :]).reshape(sel_ids.shape[0], SEL * TILE)
    key_live = jnp.repeat(live_mask, TILE, axis=1)
    allowed = key_live[:, None, None, :] & (key_pos[:, None, None, :] <= query_pos[:, None, :, None])
    scores = jnp.einsum('gqhd,gnd->ghqn', query_blk, key_sel) * inv_root
    masked = jnp.where(allowed, scores, -jnp.inf)
    row_max = jnp.max(masked, axis=3, keepdims=True)
    raised = jnp.where(allowed, jnp.exp(masked - row_max), 0.0)
    prob_rows = raised / jnp.sum(raised, axis=3, keepdims=True)
    weights = lax.optimization_barrier(prob_rows.astype(jnp.bfloat16)).astype(jnp.float32)
    d_prob = jnp.einsum('gqhd,gnd->ghqn', dout_blk, value_sel)
    row_delta = jnp.sum(prob_rows * d_prob, axis=3, keepdims=True)
    dscore = lax.optimization_barrier((prob_rows * (d_prob - row_delta)).astype(jnp.bfloat16)).astype(jnp.float32)
    grad_q = jnp.einsum('ghqn,gnd->gqhd', dscore, key_sel) * inv_root
    grad_k = jnp.einsum('ghqn,gqhd->gnd', dscore, query_blk) * inv_root
    grad_v = jnp.einsum('ghqn,gqhd->gnd', weights, dout_blk)
    return grad_q, grad_k, grad_v


def reference(queries, keyvals, selected, d_out):
    live_all = live_slots(selected)
    rounds = BLOCKS // BLK_DEV
    query_all = queries.astype(jnp.float32).reshape(BLOCKS, TILE, HEADS, DH)
    dout_all = d_out.astype(jnp.float32).reshape(BLOCKS, TILE, HEADS, DH)
    kv_all = keyvals.astype(jnp.float32).reshape(BLOCKS, TILE, KV_HEADS, 2, DH)
    grad_q_parts = []
    grad_kv_parts = []
    for kv_head in range(KV_HEADS):
        key_tiles = kv_all[:, :, kv_head, 0, :]
        value_tiles = kv_all[:, :, kv_head, 1, :]
        query_grp = query_all[:, :, kv_head * GROUP:(kv_head + 1) * GROUP, :]
        dout_grp = dout_all[:, :, kv_head * GROUP:(kv_head + 1) * GROUP, :]

        def step(totals, step_index):
            first_row = (step_index * BLK_DEV).astype(jnp.int32)
            sel_blk = lax.dynamic_slice_in_dim(selected, first_row, BLK_DEV, 0)
            live_blk = lax.dynamic_slice_in_dim(live_all, first_row, BLK_DEV, 0)
            query_blk = lax.dynamic_slice_in_dim(query_grp, first_row, BLK_DEV, 0)
            dout_blk = lax.dynamic_slice_in_dim(dout_grp, first_row, BLK_DEV, 0)
            key_sel = key_tiles[sel_blk].reshape(BLK_DEV, SEL * TILE, DH)
            value_sel = value_tiles[sel_blk].reshape(BLK_DEV, SEL * TILE, DH)
            block_ids = first_row + jnp.arange(BLK_DEV, dtype=jnp.int32)
            grad_q, grad_k, grad_v = attend_tiles(query_blk, dout_blk, key_sel, value_sel, live_blk, block_ids, sel_blk)
            key_total, value_total = totals
            key_total = key_total.at[sel_blk].add(grad_k.reshape(BLK_DEV, SEL, TILE, DH))
            value_total = value_total.at[sel_blk].add(grad_v.reshape(BLK_DEV, SEL, TILE, DH))
            return (key_total, value_total), grad_q

        start_sums = (jnp.zeros((BLOCKS, TILE, DH), jnp.float32), jnp.zeros((BLOCKS, TILE, DH), jnp.float32))
        (key_total, value_total), grad_q_all = lax.scan(step, start_sums, jnp.arange(rounds, dtype=jnp.int32))
        grad_q_parts.append(grad_q_all.reshape(SEQ_LEN, GROUP, DH))
        grad_kv_parts.append(jnp.stack([key_total.reshape(SEQ_LEN, DH), value_total.reshape(SEQ_LEN, DH)], axis=1))
    grad_queries = jnp.concatenate(grad_q_parts, axis=1).astype(jnp.bfloat16)
    grad_kv = jnp.concatenate(grad_kv_parts, axis=1).astype(jnp.bfloat16)
    return grad_queries, grad_kv
```

```python
import functools
import math

import jax
import jax.numpy as jnp
from jax import lax
from jax.experimental import pallas as pl
from jax.experimental.pallas import tpu as pltpu
from jax.sharding import PartitionSpec as P

TILE = 64
SEL = 16
CAP = 3
PACK = 4
MOST_FAR = 8
LOW = -1e30
HIGH = 1e30
NT = (((1,), (1,)), ((), ()))
TN = (((0,), (0,)), ((), ()))


def swap_pair(block):
    count = lax.axis_size("head")
    return lax.ppermute(block, "head", [(h, h ^ 1) for h in range(count)])


def tile_rows(index):
    return pl.ds(pl.multiple_of(index * TILE, TILE), TILE)


def take_tiles(ref, half, picks):
    return jnp.concatenate([ref[half, tile_rows(t), :] for t in picks], axis=0)


def dot(a, b, dims=(((1,), (0,)), ((), ()))):
    return lax.dot_general(a, b, dims, preferred_element_type=jnp.float32)


def fold(x, op):
    parts = [x[8 * i : 8 * i + 8] for i in range(TILE // 8)]
    while len(parts) > 1:
        parts = [op(parts[i], parts[i + 1]) for i in range(0, len(parts), 2)]
    return parts[0]


def mask_diagonal(x, is_first, group):
    key = lax.broadcasted_iota(jnp.int32, (TILE, x.shape[1]), 0)
    query = lax.broadcasted_iota(jnp.int32, (TILE, x.shape[1]), 1) // group
    return jnp.where((key <= query) | jnp.logical_not(is_first), x, LOW)


def lay_halves(par_ref, mine_ref, theirs_ref, kv_ref):
    par = par_ref[0]
    kv_ref[par] = mine_ref[...]
    kv_ref[1 - par] = theirs_ref[...]


def own_stats(scale, group, list_ref, par_ref, q_ref, do_ref, mine_ref, theirs_ref, st_ref, kv_ref):
    b = pl.program_id(0)

    @pl.when(b == 0)
    def _():
        lay_halves(par_ref, mine_ref, theirs_ref, kv_ref)

    count = list_ref[b, SEL]
    q = q_ref[...]
    do = do_ref[...]
    rows = q.shape[0]

    def chunk(c, carry):
        top, total, dotted = carry
        picks = [list_ref[b, c * PACK + i] for i in range(PACK)]
        real = [c * PACK + i < count for i in range(PACK)]
        x = dot(take_tiles(kv_ref, 0, picks), q, NT) * scale
        xs = [x[i * TILE : (i + 1) * TILE] for i in range(PACK)]
        xs[0] = mask_diagonal(xs[0], c == 0, group)
        new = top
        for i in range(PACK):
            new = jnp.maximum(new, jnp.where(real[i], fold(xs[i], jnp.maximum), LOW))
        new = jnp.broadcast_to(jnp.max(new, axis=0, keepdims=True), new.shape)
        fade = jnp.exp2(top - new)
        total, dotted = total * fade, dotted * fade
        dp = dot(take_tiles(kv_ref, 1, picks), do, NT)
        for i in range(PACK):
            base = jnp.where(real[i], new, HIGH)[0:1]
            e = jnp.exp2(xs[i] - base)
            total = total + fold(e, jnp.add)
            dotted = dotted + fold(e * dp[i * TILE : (i + 1) * TILE], jnp.add)
        return new, total, dotted

    zero = jnp.zeros((8, rows), jnp.float32)
    top, total, dotted = lax.fori_loop(
        0, pl.cdiv(count, PACK), chunk, (jnp.full((8, rows), LOW, jnp.float32), zero, zero)
    )
    st_ref[0] = top
    st_ref[1] = total
    st_ref[2] = dotted


def add_grads(acc_ref, picks, gk, gv):
    for i, t in enumerate(picks):
        acc_ref[0, tile_rows(t), :] += gk[i * TILE : (i + 1) * TILE]
        acc_ref[1, tile_rows(t), :] += gv[i * TILE : (i + 1) * TILE]


def far_grads(
    scale, inv_root, list_ref, par_ref, st_ref, q_ref, do_ref, mine_ref, theirs_ref,
    fin_ref, dq_ref, keep_ref, send_ref, kv_ref, acc_ref, x_ref, dp_ref,
):
    b = pl.program_id(0)

    @pl.when(b == 0)
    def _():
        lay_halves(par_ref, mine_ref, theirs_ref, kv_ref)
        acc_ref[...] = jnp.zeros_like(acc_ref)

    count = list_ref[b, SEL]
    chunks = pl.cdiv(count, PACK)
    q = q_ref[...]
    do = do_ref[...]
    span = PACK * TILE

    def chosen(c):
        return (
            [list_ref[b, c * PACK + i] for i in range(PACK)],
            [c * PACK + i < count for i in range(PACK)],
        )

    def score(c, top):
        picks, real = chosen(c)
        x = dot(take_tiles(kv_ref, 0, picks), q, NT) * scale
        x_ref[pl.ds(pl.multiple_of(c * span, span), span), :] = x
        dp_ref[pl.ds(pl.multiple_of(c * span, span), span), :] = dot(
            take_tiles(kv_ref, 1, picks), do, NT
        )
        for i in range(PACK):
            part = fold(x[i * TILE : (i + 1) * TILE], jnp.maximum)
            top = jnp.maximum(top, jnp.where(real[i], part, LOW))
        return top

    old = st_ref[0]
    top = lax.fori_loop(0, chunks, score, old)
    top = jnp.broadcast_to(jnp.max(top, axis=0, keepdims=True), top.shape)
    fade = jnp.exp2(old - top)

    def gather(c, carry):
        total, dotted = carry
        _, real = chosen(c)
        for i in range(PACK):
            at = pl.ds(pl.multiple_of(c * span + i * TILE, TILE), TILE)
            base = jnp.where(real[i], top, HIGH)[0:1]
            e = jnp.exp2(x_ref[at, :] - base)
            total = total + fold(e, jnp.add)
            dotted = dotted + fold(e * dp_ref[at, :], jnp.add)
        return total, dotted

    total, dotted = lax.fori_loop(0, chunks, gather, (st_ref[1] * fade, st_ref[2] * fade))
    total = jnp.sum(total, axis=0, keepdims=True)
    dotted = jnp.sum(dotted, axis=0, keepdims=True)
    level = top[0:1] + jnp.log2(total)
    delta = dotted / total
    fin_ref[0] = jnp.broadcast_to(level, top.shape)
    fin_ref[1] = jnp.broadcast_to(delta, top.shape)
    dq_ref[...] = jnp.zeros_like(dq_ref)

    def spread(c, _):
        picks, real = chosen(c)
        ps, dss = [], []
        for i in range(PACK):
            at = pl.ds(pl.multiple_of(c * span + i * TILE, TILE), TILE)
            p = jnp.exp2(x_ref[at, :] - jnp.where(real[i], level, HIGH))
            ps.append(p.astype(jnp.bfloat16))
            dss.append((p * (dp_ref[at, :] - delta)).astype(jnp.bfloat16))
        p, ds = jnp.concatenate(ps, axis=0), jnp.concatenate(dss, axis=0)
        add_grads(acc_ref, picks, dot(ds, q), dot(p, do))
        dq_ref[...] += dot(take_tiles(kv_ref, 0, picks), ds, TN)
        return 0

    lax.fori_loop(0, chunks, spread, 0)

    @pl.when(b == pl.num_programs(0) - 1)
    def _():
        par = par_ref[0]
        keep_ref[...] = acc_ref[par] * jnp.where(par == 0, inv_root, 1.0)
        send_ref[...] = acc_ref[1 - par] * jnp.where(par == 0, 1.0, inv_root)


def own_grads(
    scale, inv_root, group, list_ref, par_ref, fin_ref, part_ref, q_ref, do_ref, mine_ref, theirs_ref,
    out_ref, keep_ref, send_ref, kv_ref, acc_ref, dq_ref,
):
    b = pl.program_id(0)

    @pl.when(b == 0)
    def _():
        lay_halves(par_ref, mine_ref, theirs_ref, kv_ref)
        acc_ref[...] = jnp.zeros_like(acc_ref)

    count = list_ref[b, SEL]
    q = q_ref[...]
    do = do_ref[...]
    dq_ref[...] = part_ref[...]
    level = fin_ref[0][0:1]
    delta = fin_ref[1][0:1]

    def spread(c, _):
        picks = [list_ref[b, c * PACK + i] for i in range(PACK)]
        keys = take_tiles(kv_ref, 0, picks)
        x = dot(keys, q, NT) * scale
        dp = dot(take_tiles(kv_ref, 1, picks), do, NT)
        ps, dss = [], []
        for i in range(PACK):
            xi = x[i * TILE : (i + 1) * TILE]
            if i == 0:
                xi = mask_diagonal(xi, c == 0, group)
            p = jnp.exp2(xi - jnp.where(c * PACK + i < count, level, HIGH))
            ps.append(p.astype(jnp.bfloat16))
            dss.append((p * (dp[i * TILE : (i + 1) * TILE] - delta)).astype(jnp.bfloat16))
        p, ds = jnp.concatenate(ps, axis=0), jnp.concatenate(dss, axis=0)
        add_grads(acc_ref, picks, dot(ds, q), dot(p, do))
        dq_ref[...] += dot(keys, ds, TN)
        return 0

    lax.fori_loop(0, pl.cdiv(count, PACK), spread, 0)
    out_ref[...] = (dq_ref[...].T * inv_root).astype(out_ref.dtype)

    @pl.when(b == pl.num_programs(0) - 1)
    def _():
        par = par_ref[0]
        keep_ref[...] = acc_ref[par] * jnp.where(par == 0, inv_root, 1.0)
        send_ref[...] = acc_ref[1 - par] * jnp.where(par == 0, 1.0, inv_root)


def join_grads(home_ref, keep_ref, other_ref, came_ref, out_ref, acc_ref):
    acc_ref[...] = keep_ref[...] + other_ref[...]
    for i in range(home_ref.shape[0]):
        t = home_ref[i]

        @pl.when(t >= 0)
        def _():
            acc_ref[tile_rows(t), :] += came_ref[pl.ds(i * TILE, TILE), :].astype(jnp.float32)

    out_ref[...] = acc_ref[...].astype(out_ref.dtype)


def before(flags):
    n = flags.shape[1]
    earlier = jnp.arange(n)[None, :] < jnp.arange(n)[:, None]
    return jnp.sum((flags[:, None, :] & earlier[None]).astype(jnp.int32), axis=2)


def packed_list(flags, values):
    place = before(flags)
    slots = jnp.arange(SEL)
    hit = flags[:, :, None] & (place[:, :, None] == slots[None, None, :])
    packed = jnp.sum(jnp.where(hit, values[:, :, None], 0), axis=1)
    return jnp.concatenate([packed, jnp.sum(flags.astype(jnp.int32), axis=1, keepdims=True)], axis=1)


def whole(shape):
    return pl.BlockSpec(shape, lambda b, *_: (0,) * len(shape), pipeline_mode=pl.Buffered(1))


def on_device(queries, keyvals, selected, d_out):
    tok_rows, heads, dim = queries.shape
    blocks = tok_rows // TILE
    shards = lax.axis_size("seq")
    me = lax.axis_index("seq")
    par = (lax.axis_index("head") % 2).astype(jnp.int32).reshape(1)
    inv_root = dim**-0.5
    scale = inv_root / math.log(2.0)
    rows = TILE * heads
    far = shards * CAP
    f32 = jnp.float32

    mine = keyvals[:, 0, :]
    theirs = swap_pair(mine)

    owner = selected // blocks
    matches = selected[:, :, None] == jnp.arange(shards * blocks)[None, None, :]
    wanted = jnp.any(matches, axis=(0, 1)).reshape(shards, blocks)
    wanted = wanted & (jnp.arange(shards) != me)[:, None]
    rank = before(wanted)
    spots = jnp.arange(CAP)
    placed = wanted[:, :, None] & (rank[:, :, None] == spots[None, None, :])
    asked = jnp.sum(jnp.where(placed, jnp.arange(1, blocks + 1)[None, :, None], 0), axis=1) - 1
    home = lax.all_to_all(asked, "seq", split_axis=0, concat_axis=0, tiled=True).reshape(far)
    reply = mine.reshape(blocks, TILE, dim)[jnp.clip(home, 0, blocks - 1)].reshape(far * TILE, dim)
    far_mine = lax.all_to_all(reply, "seq", split_axis=0, concat_axis=0, tiled=True)
    far_theirs = swap_pair(far_mine)

    sel = jnp.concatenate([selected[:, 1:2], selected[:, :1], selected[:, 2:]], axis=1)
    slots = jnp.arange(SEL)
    repeats = (sel[:, :, None] == sel[:, None, :]) & (slots[None, :] < slots[:, None])[None]
    live = jnp.logical_not(jnp.any(repeats, axis=2))
    sel_owner = sel // blocks
    hits = sel[:, :, None] == jnp.arange(shards * blocks)[None, None, :]
    rank_of = jnp.sum(jnp.where(hits, rank.reshape(-1)[None, None, :], 0), axis=2)
    own_list = packed_list(live & (sel_owner == me), sel % blocks)
    far_list = packed_list(live & (sel_owner != me), sel_owner * CAP + rank_of)

    q2 = queries.reshape(blocks * rows, dim)
    do2 = d_out.reshape(blocks * rows, dim)
    blk = pl.BlockSpec((rows, dim), lambda b, *_: (b, 0))
    stat = pl.BlockSpec((None, 3, 8, rows), lambda b, *_: (b, 0, 0, 0))
    fin = pl.BlockSpec((None, 2, 8, rows), lambda b, *_: (b, 0, 0, 0))
    part = pl.BlockSpec((None, dim, rows), lambda b, *_: (b, 0, 0))
    params = pltpu.CompilerParams(
        dimension_semantics=("arbitrary",), vmem_limit_bytes=40 * 1024 * 1024
    )
    one = 2 * rows * TILE * dim

    stats = pl.pallas_call(
        functools.partial(own_stats, scale, heads),
        out_shape=jax.ShapeDtypeStruct((blocks, 3, 8, rows), f32),
        grid_spec=pltpu.PrefetchScalarGridSpec(
            num_scalar_prefetch=2,
            grid=(blocks,),
            in_specs=[blk, blk, whole((tok_rows, dim)), whole((tok_rows, dim))],
            out_specs=stat,
            scratch_shapes=[pltpu.VMEM((2, tok_rows, dim), jnp.bfloat16)],
        ),
        compiler_params=params,
        cost_estimate=pl.CostEstimate(
            flops=2 * one * blocks * 8, bytes_accessed=2 * tok_rows * heads * dim * 2, transcendentals=0
        ),
        name="own_stats",
    )(own_list, par, q2, do2, mine, theirs)

    final, dq_part, far_keep, far_send = pl.pallas_call(
        functools.partial(far_grads, scale, inv_root),
        out_shape=(
            jax.ShapeDtypeStruct((blocks, 2, 8, rows), f32),
            jax.ShapeDtypeStruct((blocks, dim, rows), f32),
            jax.ShapeDtypeStruct((far * TILE, dim), f32),
            jax.ShapeDtypeStruct((far * TILE, dim), f32),
        ),
        grid_spec=pltpu.PrefetchScalarGridSpec(
            num_scalar_prefetch=2,
            grid=(blocks,),
            in_specs=[stat, blk, blk, whole((far * TILE, dim)), whole((far * TILE, dim))],
            out_specs=(fin, part, whole((far * TILE, dim)), whole((far * TILE, dim))),
            scratch_shapes=[
                pltpu.VMEM((2, far * TILE, dim), jnp.bfloat16),
                pltpu.VMEM((2, far * TILE, dim), f32),
                pltpu.VMEM((MOST_FAR * TILE, rows), f32),
                pltpu.VMEM((MOST_FAR * TILE, rows), f32),
            ],
        ),
        compiler_params=params,
        cost_estimate=pl.CostEstimate(
            flops=5 * one * blocks * 6, bytes_accessed=4 * tok_rows * heads * dim * 2, transcendentals=0
        ),
        name="far_grads",
    )(far_list, par, stats, q2, do2, far_mine, far_theirs)

    back = (far_keep + swap_pair(far_send)).astype(jnp.bfloat16)
    came = lax.all_to_all(back, "seq", split_axis=0, concat_axis=0, tiled=True)

    grad_q, own_keep, own_send = pl.pallas_call(
        functools.partial(own_grads, scale, inv_root, heads),
        out_shape=(
            jax.ShapeDtypeStruct((blocks * rows, dim), jnp.bfloat16),
            jax.ShapeDtypeStruct((tok_rows, dim), f32),
            jax.ShapeDtypeStruct((tok_rows, dim), f32),
        ),
        grid_spec=pltpu.PrefetchScalarGridSpec(
            num_scalar_prefetch=2,
            grid=(blocks,),
            in_specs=[fin, part, blk, blk, whole((tok_rows, dim)), whole((tok_rows, dim))],
            out_specs=(blk, whole((tok_rows, dim)), whole((tok_rows, dim))),
            scratch_shapes=[
                pltpu.VMEM((2, tok_rows, dim), jnp.bfloat16),
                pltpu.VMEM((2, tok_rows, dim), f32),
                pltpu.VMEM((dim, rows), f32),
            ],
        ),
        compiler_params=params,
        cost_estimate=pl.CostEstimate(
            flops=5 * one * blocks * 8, bytes_accessed=5 * tok_rows * heads * dim * 2, transcendentals=0
        ),
        name="own_grads",
    )(own_list, par, final, dq_part, q2, do2, mine, theirs)

    other = swap_pair(own_send)
    grad_kv = pl.pallas_call(
        join_grads,
        out_shape=jax.ShapeDtypeStruct((tok_rows, dim), jnp.bfloat16),
        in_specs=[pl.BlockSpec(memory_space=pltpu.SMEM)] + [pl.BlockSpec(memory_space=pltpu.VMEM)] * 3,
        out_specs=pl.BlockSpec(memory_space=pltpu.VMEM),
        scratch_shapes=[pltpu.VMEM((tok_rows, dim), f32)],
        name="join_grads",
    )(home, own_keep, other, came)
    return (grad_q.reshape(tok_rows, heads, dim), grad_kv.reshape(tok_rows, 1, dim))


def solution(mesh):
    in_specs = (
        P("seq", "head", None),
        P("seq", "head", None),
        P("seq", None),
        P("seq", "head", None),
    )
    out_specs = (P("seq", "head", None), P("seq", "head", None))
    return jax.shard_map(
        on_device, mesh=mesh, in_specs=in_specs, out_specs=out_specs, check_vma=False
    )
```

```python
import functools
import math

import jax
import jax.numpy as jnp
from jax import lax
from jax.experimental import pallas as pl
from jax.experimental.pallas import tpu as pltpu
from jax.sharding import PartitionSpec as P

TILE = 64
SEL = 16
CAP = 3
WIDE = 8
OWN_SIZES = (2, 4, 6)
FAR_SIZES = (4, 7, 8)
STEP = 2
LOW = -1e30
HIGH = 1e30
RISE = 64.0
NT = (((1,), (1,)), ((), ()))
TN = (((0,), (0,)), ((), ()))


def swap_pair(block):
    count = lax.axis_size("head")
    return lax.ppermute(block, "head", [(h, h ^ 1) for h in range(count)])


def tile_rows(index):
    return pl.ds(pl.multiple_of(index * TILE, TILE), TILE)


def span(index, size):
    return pl.ds(pl.multiple_of(index * size, size), size)


def dot(a, b, dims=(((1,), (0,)), ((), ()))):
    return lax.dot_general(a, b, dims, preferred_element_type=jnp.float32)


def fold(x, op):
    parts = [x[8 * i : 8 * i + 8] for i in range(TILE // 8)]
    while len(parts) > 1:
        parts = [op(parts[i], parts[i + 1]) for i in range(0, len(parts), 2)]
    return parts[0]


def mask_diagonal(x, is_first, group):
    key = lax.broadcasted_iota(jnp.int32, (TILE, x.shape[1]), 0)
    query = lax.broadcasted_iota(jnp.int32, (TILE, x.shape[1]), 1) // group
    return jnp.where((key <= query) | jnp.logical_not(is_first), x, LOW)


def lay_halves(par_ref, mine_ref, theirs_ref, kv_ref):
    par = par_ref[0]
    kv_ref[par] = mine_ref[...]
    kv_ref[1 - par] = theirs_ref[...]


def each_block(body):
    def run(j, _):
        body(pl.program_id(0) * STEP + j, j)
        return 0

    lax.fori_loop(0, STEP, run, 0)


def pick(list_ref, b, start, size):
    count = list_ref[b, SEL]
    return (
        [list_ref[b, start + i] for i in range(size)],
        [start + i < count for i in range(size)],
    )


def part(i):
    return slice(i * TILE, (i + 1) * TILE)


def load_tiles(kv_ref, k_ref, v_ref, picks):
    for i, t in enumerate(picks):
        k_ref[part(i)] = kv_ref[0, tile_rows(t), :]
        v_ref[part(i)] = kv_ref[1, tile_rows(t), :]


def by_size(left, sizes, run):
    for low, size in zip((0,) + sizes[:-1], sizes, strict=True):

        @pl.when((left > low) & (left <= size))
        def _():
            run(size)


def in_parts(count, run):
    wide = (count + 1) // WIDE

    def full(c, _):
        run(c * WIDE, WIDE)
        return 0

    lax.fori_loop(0, wide, full, 0)
    by_size(count - wide * WIDE, OWN_SIZES, lambda size: run(wide * WIDE, size))


def own_stats(
    scale, group, list_ref, par_ref, q_ref, do_ref, mine_ref, theirs_ref, st_ref, kv_ref, k_ref, v_ref
):
    rows = q_ref.shape[0] // STEP

    @pl.when(pl.program_id(0) == 0)
    def _():
        lay_halves(par_ref, mine_ref, theirs_ref, kv_ref)

    def block(b, j):
        zero = jnp.zeros((8, rows), jnp.float32)
        st_ref[j, 0] = jnp.full((8, rows), LOW, jnp.float32)
        st_ref[j, 1] = zero
        st_ref[j, 2] = zero

        def run(start, size):
            picks, real = pick(list_ref, b, start, size)
            load_tiles(kv_ref, k_ref, v_ref, picks)
            x = dot(k_ref[: size * TILE], q_ref[span(j, rows), :], NT) * scale
            xs = [x[part(i)] for i in range(size)]
            xs[0] = mask_diagonal(xs[0], start == 0, group)
            top = st_ref[j, 0]
            new = top
            for i in range(size):
                new = jnp.maximum(new, jnp.where(real[i], fold(xs[i], jnp.maximum), LOW))
            new = jnp.broadcast_to(jnp.max(new, axis=0, keepdims=True), new.shape)
            fade = jnp.exp2(top - new)
            total, dotted = st_ref[j, 1] * fade, st_ref[j, 2] * fade
            dp = dot(v_ref[: size * TILE], do_ref[span(j, rows), :], NT)
            for i in range(size):
                base = jnp.where(real[i], new, HIGH)[0:1]
                e = jnp.exp2(xs[i] - base)
                total = total + fold(e, jnp.add)
                dotted = dotted + fold(e * dp[part(i)], jnp.add)
            st_ref[j, 0] = new
            st_ref[j, 1] = total
            st_ref[j, 2] = dotted

        in_parts(list_ref[b, SEL], run)

    each_block(block)


def add_grads(acc_ref, picks, gk, gv):
    for i, t in enumerate(picks):
        acc_ref[0, tile_rows(t), :] += gk[part(i)]
        acc_ref[1, tile_rows(t), :] += gv[part(i)]


def leave_grads(inv_root, par_ref, acc_ref, keep_ref, send_ref):
    @pl.when(pl.program_id(0) == pl.num_programs(0) - 1)
    def _():
        par = par_ref[0]
        keep = acc_ref[par] * jnp.where(par == 0, inv_root, 1.0)
        send = acc_ref[1 - par] * jnp.where(par == 0, 1.0, inv_root)
        keep_ref[...] = keep.astype(keep_ref.dtype)
        send_ref[...] = send.astype(send_ref.dtype)


def far_grads(
    scale, inv_root, list_ref, par_ref, st_ref, q_ref, do_ref, mine_ref, theirs_ref,
    fin_ref, dq_ref, keep_ref, send_ref,
    kv_ref, acc_ref, e_ref, dp_ref, sum_ref, k_ref, v_ref, p_ref, ds_ref,
):
    rows = q_ref.shape[0] // STEP

    @pl.when(pl.program_id(0) == 0)
    def _():
        lay_halves(par_ref, mine_ref, theirs_ref, kv_ref)
        acc_ref[...] = jnp.zeros_like(acc_ref)

    def block(b, j):
        count = list_ref[b, SEL]
        q_at = span(j, rows)

        def read(start, size):
            picks, real = pick(list_ref, b, start, size)
            load_tiles(kv_ref, k_ref, v_ref, picks)
            x = dot(k_ref[: size * TILE], q_ref[q_at, :], NT) * scale
            dp = dot(v_ref[: size * TILE], do_ref[q_at, :], NT)
            base, total, dotted, top = sum_ref[0], sum_ref[1], sum_ref[2], sum_ref[3]
            for i in range(size):
                to = tile_rows(start + i)
                top = jnp.maximum(top, jnp.where(real[i], fold(x[part(i)], jnp.maximum), LOW))
                e = jnp.exp2(x[part(i)] - jnp.where(real[i], base, HIGH)[0:1])
                e_ref[to, :] = e
                dp_ref[to, :] = dp[part(i)]
                total = total + fold(e, jnp.add)
                dotted = dotted + fold(e * dp[part(i)], jnp.add)
            sum_ref[1], sum_ref[2], sum_ref[3] = total, dotted, top

        old = st_ref[j, 0]
        sum_ref[0] = old
        sum_ref[1] = st_ref[j, 1]
        sum_ref[2] = st_ref[j, 2]
        sum_ref[3] = old
        by_size(count, FAR_SIZES, lambda size: read(0, size))

        @pl.when(jnp.max(sum_ref[3] - old) > RISE)
        def _():
            best = jnp.broadcast_to(jnp.max(sum_ref[3], axis=0, keepdims=True), old.shape)
            fade = jnp.exp2(old - best)
            sum_ref[0] = best
            sum_ref[1] = st_ref[j, 1] * fade
            sum_ref[2] = st_ref[j, 2] * fade

            def again(c, _):
                read(c * FAR_SIZES[0], FAR_SIZES[0])
                return 0

            lax.fori_loop(0, pl.cdiv(count, FAR_SIZES[0]), again, 0)

        total = jnp.sum(sum_ref[1], axis=0, keepdims=True)
        dotted = jnp.sum(sum_ref[2], axis=0, keepdims=True)
        delta = dotted / total
        ratio = 1.0 / total
        fin_ref[j, 0] = sum_ref[0] + jnp.log2(total)
        fin_ref[j, 1] = jnp.broadcast_to(delta, old.shape)

        @pl.when(count == 0)
        def _():
            dq_ref[j] = jnp.zeros(dq_ref.shape[1:], dq_ref.dtype)

        def spread(size):
            picks, _ = pick(list_ref, b, 0, size)
            n = size * TILE
            for i, t in enumerate(picks):
                k_ref[part(i)] = kv_ref[0, tile_rows(t), :]
                p = e_ref[part(i)] * ratio
                p_ref[part(i)] = p.astype(jnp.bfloat16)
                ds_ref[part(i)] = (p * (dp_ref[part(i)] - delta)).astype(jnp.bfloat16)
            add_grads(acc_ref, picks, dot(ds_ref[:n], q_ref[q_at, :]), dot(p_ref[:n], do_ref[q_at, :]))
            dq_ref[j] = dot(k_ref[:n], ds_ref[:n], TN)

        by_size(count, FAR_SIZES, spread)

    each_block(block)
    leave_grads(inv_root, par_ref, acc_ref, keep_ref, send_ref)


def own_grads(
    scale, inv_root, group, list_ref, par_ref, fin_ref, part_ref, q_ref, do_ref, mine_ref, theirs_ref,
    out_ref, keep_ref, send_ref, kv_ref, acc_ref, dq_ref, k_ref, v_ref, p_ref, ds_ref,
):
    rows = q_ref.shape[0] // STEP

    @pl.when(pl.program_id(0) == 0)
    def _():
        lay_halves(par_ref, mine_ref, theirs_ref, kv_ref)
        acc_ref[...] = jnp.zeros_like(acc_ref)

    def block(b, j):
        q_at = span(j, rows)
        dq_ref[...] = part_ref[j]

        def spread(start, size):
            picks, real = pick(list_ref, b, start, size)
            n = size * TILE
            load_tiles(kv_ref, k_ref, v_ref, picks)
            level = fin_ref[j, 0, 0:1]
            delta = fin_ref[j, 1, 0:1]
            x = dot(k_ref[:n], q_ref[q_at, :], NT) * scale
            dp = dot(v_ref[:n], do_ref[q_at, :], NT)
            for i in range(size):
                xi = mask_diagonal(x[part(i)], start == 0, group) if i == 0 else x[part(i)]
                p = jnp.exp2(xi - jnp.where(real[i], level, HIGH))
                p_ref[part(i)] = p.astype(jnp.bfloat16)
                ds_ref[part(i)] = (p * (dp[part(i)] - delta)).astype(jnp.bfloat16)
            add_grads(acc_ref, picks, dot(ds_ref[:n], q_ref[q_at, :]), dot(p_ref[:n], do_ref[q_at, :]))
            dq_ref[...] += dot(k_ref[:n], ds_ref[:n], TN)

        in_parts(list_ref[b, SEL], spread)
        out_ref[q_at, :] = (dq_ref[...] * inv_root).astype(out_ref.dtype).T

    each_block(block)
    leave_grads(inv_root, par_ref, acc_ref, keep_ref, send_ref)


def fill_reply(home_ref, mine_ref, reply_ref):
    cap = home_ref.shape[2]
    for i in range(home_ref.shape[0] * cap):
        t = jnp.maximum(home_ref[i // cap, 0, i % cap], 0)
        reply_ref[i * TILE : (i + 1) * TILE] = mine_ref[tile_rows(t), :]


def join_grads(home_ref, keep_ref, other_ref, came_ref, out_ref, acc_ref):
    cap = home_ref.shape[2]
    acc_ref[...] = keep_ref[...] + other_ref[...]
    for i in range(home_ref.shape[0] * cap):
        t = home_ref[i // cap, 0, i % cap]

        @pl.when(t >= 0)
        def _():
            acc_ref[tile_rows(t), :] += came_ref[i * TILE : (i + 1) * TILE].astype(jnp.float32)

    out_ref[...] = acc_ref[...].astype(out_ref.dtype)


def before(flags):
    n = flags.shape[1]
    earlier = jnp.arange(n)[None, :] < jnp.arange(n)[:, None]
    return jnp.sum((flags[:, None, :] & earlier[None]).astype(jnp.int32), axis=2)


def packed_list(flags, values):
    place = before(flags)
    slots = jnp.arange(SEL)
    hit = flags[:, :, None] & (place[:, :, None] == slots[None, None, :])
    packed = jnp.sum(jnp.where(hit, values[:, :, None], 0), axis=1)
    return jnp.concatenate([packed, jnp.sum(flags.astype(jnp.int32), axis=1, keepdims=True)], axis=1)


def whole(shape):
    return pl.BlockSpec(shape, lambda b, *_: (0,) * len(shape), pipeline_mode=pl.Buffered(1))


def on_device(queries, keyvals, selected, d_out):
    tok_rows, heads, dim = queries.shape
    blocks = tok_rows // TILE
    shards = lax.axis_size("seq")
    me = lax.axis_index("seq")
    par = (lax.axis_index("head") % 2).astype(jnp.int32).reshape(1)
    inv_root = dim**-0.5
    scale = inv_root / math.log(2.0)
    rows = TILE * heads
    far = shards * CAP
    f32 = jnp.float32

    mine = keyvals[:, 0, :]
    theirs = swap_pair(mine)

    owner = selected // blocks
    matches = selected[:, :, None] == jnp.arange(shards * blocks)[None, None, :]
    wanted = jnp.any(matches, axis=(0, 1)).reshape(shards, blocks)
    wanted = wanted & (jnp.arange(shards) != me)[:, None]
    rank = before(wanted)
    spots = jnp.arange(CAP)
    placed = wanted[:, :, None] & (rank[:, :, None] == spots[None, None, :])
    asked = jnp.sum(jnp.where(placed, jnp.arange(1, blocks + 1)[None, :, None], 0), axis=1) - 1
    home = lax.all_to_all(asked[:, None, :], "seq", split_axis=0, concat_axis=0, tiled=True)
    in_smem = pl.BlockSpec(memory_space=pltpu.SMEM)
    in_vmem = pl.BlockSpec(memory_space=pltpu.VMEM)
    reply = pl.pallas_call(
        fill_reply,
        out_shape=jax.ShapeDtypeStruct((far * TILE, dim), jnp.bfloat16),
        in_specs=[in_smem, in_vmem],
        out_specs=in_vmem,
        compiler_params=pltpu.CompilerParams(vmem_limit_bytes=60 * 1024 * 1024),
        name="fill_reply",
    )(home, mine)
    far_mine = lax.all_to_all(reply, "seq", split_axis=0, concat_axis=0, tiled=True)

    sel = jnp.concatenate([selected[:, 1:2], selected[:, :1], selected[:, 2:]], axis=1)
    slots = jnp.arange(SEL)
    repeats = (sel[:, :, None] == sel[:, None, :]) & (slots[None, :] < slots[:, None])[None]
    live = jnp.logical_not(jnp.any(repeats, axis=2))
    sel_owner = sel // blocks
    hits = sel[:, :, None] == jnp.arange(shards * blocks)[None, None, :]
    rank_of = jnp.sum(jnp.where(hits, rank.reshape(-1)[None, None, :], 0), axis=2)
    own_list = packed_list(live & (sel_owner == me), sel % blocks)
    far_list = packed_list(live & (sel_owner != me), sel_owner * CAP + rank_of)

    q2 = queries.reshape(blocks * rows, dim)
    do2 = d_out.reshape(blocks * rows, dim)
    blk = pl.BlockSpec((STEP * rows, dim), lambda b, *_: (b, 0))
    stat = pl.BlockSpec((STEP, 3, 8, rows), lambda b, *_: (b, 0, 0, 0))
    fin = pl.BlockSpec((STEP, 2, 8, rows), lambda b, *_: (b, 0, 0, 0))
    part_dq = pl.BlockSpec((STEP, dim, rows), lambda b, *_: (b, 0, 0))
    params = pltpu.CompilerParams(
        dimension_semantics=("arbitrary",), vmem_limit_bytes=60 * 1024 * 1024
    )
    one = 2 * rows * TILE * dim
    bf16 = jnp.bfloat16
    own_rows, far_rows = (tok_rows, dim), (far * TILE, dim)
    some_keys = [pltpu.VMEM((WIDE * TILE, dim), bf16)] * 2
    some_probs = [pltpu.VMEM((WIDE * TILE, rows), bf16)] * 2

    stats = pl.pallas_call(
        functools.partial(own_stats, scale, heads),
        out_shape=jax.ShapeDtypeStruct((blocks, 3, 8, rows), f32),
        grid_spec=pltpu.PrefetchScalarGridSpec(
            num_scalar_prefetch=2,
            grid=(blocks // STEP,),
            in_specs=[blk, blk, whole(own_rows), whole(own_rows)],
            out_specs=stat,
            scratch_shapes=[pltpu.VMEM((2,) + own_rows, bf16)] + some_keys,
        ),
        compiler_params=params,
        cost_estimate=pl.CostEstimate(
            flops=2 * one * blocks * 8, bytes_accessed=2 * tok_rows * heads * dim * 2, transcendentals=0
        ),
        name="own_stats",
    )(own_list, par, q2, do2, mine, theirs)

    far_mine, stats = lax.optimization_barrier((far_mine, stats))
    far_theirs = swap_pair(far_mine)

    final, dq_part, far_keep, far_send = pl.pallas_call(
        functools.partial(far_grads, scale, inv_root),
        out_shape=(
            jax.ShapeDtypeStruct((blocks, 2, 8, rows), f32),
            jax.ShapeDtypeStruct((blocks, dim, rows), f32),
            jax.ShapeDtypeStruct(far_rows, f32),
            jax.ShapeDtypeStruct(far_rows, bf16),
        ),
        grid_spec=pltpu.PrefetchScalarGridSpec(
            num_scalar_prefetch=2,
            grid=(blocks // STEP,),
            in_specs=[stat, blk, blk, whole(far_rows), whole(far_rows)],
            out_specs=(fin, part_dq, whole(far_rows), whole(far_rows)),
            scratch_shapes=[
                pltpu.VMEM((2,) + far_rows, bf16),
                pltpu.VMEM((2,) + far_rows, f32),
                pltpu.VMEM((WIDE * TILE, rows), f32),
                pltpu.VMEM((WIDE * TILE, rows), f32),
                pltpu.VMEM((4, 8, rows), f32),
            ]
            + some_keys
            + some_probs,
        ),
        compiler_params=params,
        cost_estimate=pl.CostEstimate(
            flops=5 * one * blocks * 6, bytes_accessed=4 * tok_rows * heads * dim * 2, transcendentals=0
        ),
        name="far_grads",
    )(far_list, par, stats, q2, do2, far_mine, far_theirs)

    back = (far_keep + swap_pair(far_send).astype(f32)).astype(bf16)
    came = lax.all_to_all(back, "seq", split_axis=0, concat_axis=0, tiled=True)

    grad_q, own_keep, own_send = pl.pallas_call(
        functools.partial(own_grads, scale, inv_root, heads),
        out_shape=(
            jax.ShapeDtypeStruct((blocks * rows, dim), bf16),
            jax.ShapeDtypeStruct(own_rows, f32),
            jax.ShapeDtypeStruct(own_rows, f32),
        ),
        grid_spec=pltpu.PrefetchScalarGridSpec(
            num_scalar_prefetch=2,
            grid=(blocks // STEP,),
            in_specs=[fin, part_dq, blk, blk, whole(own_rows), whole(own_rows)],
            out_specs=(blk, whole(own_rows), whole(own_rows)),
            scratch_shapes=[
                pltpu.VMEM((2,) + own_rows, bf16),
                pltpu.VMEM((2,) + own_rows, f32),
                pltpu.VMEM((dim, rows), f32),
            ]
            + some_keys
            + some_probs,
        ),
        compiler_params=params,
        cost_estimate=pl.CostEstimate(
            flops=5 * one * blocks * 8, bytes_accessed=5 * tok_rows * heads * dim * 2, transcendentals=0
        ),
        name="own_grads",
    )(own_list, par, final, dq_part, q2, do2, mine, theirs)

    other = swap_pair(own_send)
    grad_kv = pl.pallas_call(
        join_grads,
        out_shape=jax.ShapeDtypeStruct(own_rows, bf16),
        in_specs=[in_smem, in_vmem, in_vmem, in_vmem],
        out_specs=in_vmem,
        scratch_shapes=[pltpu.VMEM(own_rows, f32)],
        compiler_params=pltpu.CompilerParams(vmem_limit_bytes=60 * 1024 * 1024),
        name="join_grads",
    )(home, own_keep, other, came)
    return (grad_q.reshape(tok_rows, heads, dim), grad_kv.reshape(tok_rows, 1, dim))


def solution(mesh):
    in_specs = (
        P("seq", "head", None),
        P("seq", "head", None),
        P("seq", None),
        P("seq", "head", None),
    )
    out_specs = (P("seq", "head", None), P("seq", "head", None))
    return jax.shard_map(
        on_device, mesh=mesh, in_specs=in_specs, out_specs=out_specs, check_vma=False
    )
```

```python
import functools
import math

import jax
import jax.numpy as jnp
from jax import lax
from jax.experimental import pallas as pl
from jax.experimental.pallas import tpu as pltpu
from jax.sharding import PartitionSpec as P

TILE = 64
SEL = 16
CAP = 3
WIDE = 8
OWN_SIZES = (2, 4, 6)
FAR_SIZES = (4, 7, 8)
VMEM_LIMIT = 40 * 1024 * 1024
SMALL_LIMIT = 8 * 1024 * 1024
STEP = 4
LOW = -1e30
HIGH = 1e30
TOO_LARGE = 2.0**64
NT = (((1,), (1,)), ((), ()))
TN = (((0,), (0,)), ((), ()))


def swap_pair(block):
    count = lax.axis_size("head")
    return lax.ppermute(block, "head", [(h, h ^ 1) for h in range(count)])


def keep_in_hbm(array):
    return pltpu.with_memory_space_constraint(array, pltpu.HBM)


def tile_rows(index):
    return pl.ds(pl.multiple_of(index * TILE, TILE), TILE)


def span(index, size):
    return pl.ds(pl.multiple_of(index * size, size), size)


def dot(a, b, dims=(((1,), (0,)), ((), ()))):
    return lax.dot_general(a, b, dims, preferred_element_type=jnp.float32)


def fold(x, op):
    parts = [x[8 * i : 8 * i + 8] for i in range(TILE // 8)]
    while len(parts) > 1:
        parts = [op(parts[i], parts[i + 1]) for i in range(0, len(parts), 2)]
    return parts[0]


def places(rows, group):
    key = lax.broadcasted_iota(jnp.int32, (TILE, rows), 0)
    query = lax.broadcasted_iota(jnp.int32, (TILE, rows), 1) // group
    return key, query


def mask_diagonal(x, is_first, group):
    key, query = places(x.shape[1], group)
    return jnp.where((key <= query) | jnp.logical_not(is_first), x, LOW)


def pick_diagonal(x, group):
    key, query = places(x.shape[1], group)
    return jnp.sum(fold(jnp.where(key == query, x, 0.0), jnp.add), axis=0, keepdims=True)


def lay_halves(par_ref, mine_ref, theirs_ref, kv_ref):
    par = par_ref[0]
    kv_ref[par] = mine_ref[...]
    kv_ref[1 - par] = theirs_ref[...]


def each_block(body):
    def run(j, _):
        body(pl.program_id(0) * STEP + j, j)
        return 0

    lax.fori_loop(0, STEP, run, 0)


def pick(list_ref, b, start, size):
    count = list_ref[b, SEL]
    return (
        [list_ref[b, start + i] for i in range(size)],
        [start + i < count for i in range(size)],
    )


def part(i):
    return slice(i * TILE, (i + 1) * TILE)


def load_tiles(kv_ref, k_ref, v_ref, picks):
    for i, t in enumerate(picks):
        k_ref[part(i)] = kv_ref[0, tile_rows(t), :]
        v_ref[part(i)] = kv_ref[1, tile_rows(t), :]


def by_size(left, sizes, run):
    for low, size in zip((0,) + sizes[:-1], sizes, strict=True):

        @pl.when((left > low) & (left <= size))
        def _():
            run(size)


def in_parts(count, run):
    wide = (count + 1) // WIDE

    def full(c, _):
        run(c * WIDE, WIDE)
        return 0

    lax.fori_loop(0, wide, full, 0)
    by_size(count - wide * WIDE, OWN_SIZES, lambda size: run(wide * WIDE, size))


def sum_up(x):
    return jnp.sum(x, axis=0, keepdims=True)


def own_stats(
    scale, group, list_ref, par_ref, q_ref, do_ref, mine_ref, theirs_ref, st_ref,
    kv_ref, k_ref, v_ref, sum_ref,
):
    rows = q_ref.shape[0] // STEP

    @pl.when(pl.program_id(0) == 0)
    def _():
        lay_halves(par_ref, mine_ref, theirs_ref, kv_ref)

    def block(b, j, again=False):
        count = list_ref[b, SEL]
        q_at = span(j, rows)
        sums = sum_ref.at[j]

        def scores(start, size):
            picks, real = pick(list_ref, b, start, size)
            load_tiles(kv_ref, k_ref, v_ref, picks)
            return dot(k_ref[: size * TILE], q_ref[q_at, :], NT) * scale, real

        def run(start, size):
            x, real = scores(start, size)
            dp = dot(v_ref[: size * TILE], do_ref[q_at, :], NT)
            base = sums[0]
            if not again:
                base = jnp.where(start == 0, pick_diagonal(x[part(0)], group), base)
                sums[0] = base
            base = base[0:1]
            total, dotted = sums[1], sums[2]
            for i in range(size):
                xi = mask_diagonal(x[part(i)], start == 0, group) if i == 0 else x[part(i)]
                e = jnp.exp2(xi - jnp.where(real[i], base, HIGH))
                total = total + fold(e, jnp.add)
                dotted = dotted + fold(e * dp[part(i)], jnp.add)
            sums[1] = total
            sums[2] = dotted

        if not again:
            sums[...] = jnp.zeros_like(sums)
            in_parts(count, run)
            return

        size = OWN_SIZES[0]
        sums[0] = jnp.full(sums.shape[1:], LOW, jnp.float32)

        def look(c, _):
            x, real = scores(c * size, size)
            top = sums[0]
            for i in range(size):
                xi = mask_diagonal(x[part(i)], c == 0, group) if i == 0 else x[part(i)]
                top = jnp.maximum(top, jnp.where(real[i], fold(xi, jnp.maximum), LOW))
            sums[0] = top
            return 0

        def anew(c, _):
            run(c * size, size)
            return 0

        lax.fori_loop(0, pl.cdiv(count, size), look, 0)
        sums[0] = jnp.broadcast_to(jnp.max(sums[0], axis=0, keepdims=True), sums.shape[1:])
        sums[1] = jnp.zeros(sums.shape[1:], jnp.float32)
        sums[2] = jnp.zeros(sums.shape[1:], jnp.float32)
        lax.fori_loop(0, pl.cdiv(count, size), anew, 0)

    each_block(block)

    @pl.when(jnp.max(sum_ref[:, 1]) > TOO_LARGE)
    def _():
        each_block(functools.partial(block, again=True))

    for j in range(STEP):
        st_ref[j, 0:1] = sum_ref[j, 0, 0:1]
        st_ref[j, 1:2] = sum_up(sum_ref[j, 1])
        st_ref[j, 2:3] = sum_up(sum_ref[j, 2])


def add_grads(acc_ref, picks, gk, gv):
    for i, t in enumerate(picks):
        acc_ref[0, tile_rows(t), :] += gk[part(i)]
        acc_ref[1, tile_rows(t), :] += gv[part(i)]


def leave_grads(inv_root, par_ref, acc_ref, keep_ref, send_ref):
    @pl.when(pl.program_id(0) == pl.num_programs(0) - 1)
    def _():
        par = par_ref[0]
        keep = acc_ref[par] * jnp.where(par == 0, inv_root, 1.0)
        send = acc_ref[1 - par] * jnp.where(par == 0, 1.0, inv_root)
        keep_ref[...] = keep.astype(keep_ref.dtype)
        send_ref[...] = send.astype(send_ref.dtype)


def far_grads(
    scale, inv_root, list_ref, par_ref, st_ref, q_ref, do_ref, mine_ref, theirs_ref,
    fin_ref, dq_ref, keep_ref, send_ref,
    kv_ref, acc_ref, e_ref, dp_ref, sum_ref, k_ref, v_ref, p_ref, ds_ref,
):
    rows = q_ref.shape[0] // STEP

    @pl.when(pl.program_id(0) == 0)
    def _():
        lay_halves(par_ref, mine_ref, theirs_ref, kv_ref)
        acc_ref[...] = jnp.zeros_like(acc_ref)

    def first(b, j, again=False):
        count = list_ref[b, SEL]
        q_at = span(j, rows)
        sums = sum_ref.at[j]

        def scores(start, size):
            picks, real = pick(list_ref, b, start, size)
            load_tiles(kv_ref, k_ref, v_ref, picks)
            return dot(k_ref[: size * TILE], q_ref[q_at, :], NT) * scale, real

        def read(start, size):
            x, real = scores(start, size)
            dp = dot(v_ref[: size * TILE], do_ref[q_at, :], NT)
            base, total, dotted = sums[0, 0:1], sums[1], sums[2]
            for i in range(size):
                to = tile_rows(start + i)
                e = jnp.exp2(x[part(i)] - jnp.where(real[i], base, HIGH))
                e_ref[j, to, :] = e
                dp_ref[j, to, :] = dp[part(i)]
                total = total + fold(e, jnp.add)
                dotted = dotted + fold(e * dp[part(i)], jnp.add)
            sums[1] = total
            sums[2] = dotted

        def begin(base):
            fade = jnp.exp2(st_ref[j, 0:1] - base)
            at_top = lax.broadcasted_iota(jnp.int32, sums.shape[1:], 0) == 0
            sums[0] = jnp.broadcast_to(base, sums.shape[1:])
            sums[1] = jnp.where(at_top, st_ref[j, 1:2] * fade, 0.0)
            sums[2] = jnp.where(at_top, st_ref[j, 2:3] * fade, 0.0)

        if not again:
            begin(st_ref[j, 0:1])
            by_size(count, FAR_SIZES, lambda size: read(0, size))
            return

        size = FAR_SIZES[0]
        sums[0] = jnp.broadcast_to(st_ref[j, 0:1], sums.shape[1:])

        def look(c, _):
            x, real = scores(c * size, size)
            top = sums[0]
            for i in range(size):
                top = jnp.maximum(top, jnp.where(real[i], fold(x[part(i)], jnp.maximum), LOW))
            sums[0] = top
            return 0

        def anew(c, _):
            read(c * size, size)
            return 0

        lax.fori_loop(0, pl.cdiv(count, size), look, 0)
        begin(jnp.max(sums[0], axis=0, keepdims=True))
        lax.fori_loop(0, pl.cdiv(count, size), anew, 0)

    def second(b, j):
        count = list_ref[b, SEL]
        q_at = span(j, rows)
        total, dotted = sum_up(sum_ref[j, 1]), sum_up(sum_ref[j, 2])
        delta = dotted / total
        ratio = 1.0 / total
        fin_ref[j, 0:1] = sum_ref[j, 0, 0:1] + jnp.log2(total)
        fin_ref[j, 1:2] = delta

        @pl.when(count == 0)
        def _():
            dq_ref[j] = jnp.zeros(dq_ref.shape[1:], dq_ref.dtype)

        def spread(size):
            picks, _ = pick(list_ref, b, 0, size)
            n = size * TILE
            for i, t in enumerate(picks):
                k_ref[part(i)] = kv_ref[0, tile_rows(t), :]
                p = e_ref[j, part(i)] * ratio
                p_ref[part(i)] = p.astype(jnp.bfloat16)
                ds_ref[part(i)] = (p * (dp_ref[j, part(i)] - delta)).astype(jnp.bfloat16)
            add_grads(acc_ref, picks, dot(ds_ref[:n], q_ref[q_at, :]), dot(p_ref[:n], do_ref[q_at, :]))
            dq_ref[j] = dot(k_ref[:n], ds_ref[:n], TN).astype(dq_ref.dtype)

        by_size(count, FAR_SIZES, spread)

    each_block(first)

    @pl.when(jnp.max(sum_ref[:, 1]) > TOO_LARGE)
    def _():
        each_block(functools.partial(first, again=True))

    each_block(second)
    leave_grads(inv_root, par_ref, acc_ref, keep_ref, send_ref)


def own_grads(
    scale, inv_root, group, list_ref, par_ref, fin_ref, part_ref, q_ref, do_ref, mine_ref, theirs_ref,
    out_ref, keep_ref, send_ref, kv_ref, acc_ref, dq_ref, k_ref, v_ref, p_ref, ds_ref,
):
    rows = q_ref.shape[0] // STEP

    @pl.when(pl.program_id(0) == 0)
    def _():
        lay_halves(par_ref, mine_ref, theirs_ref, kv_ref)
        acc_ref[...] = jnp.zeros_like(acc_ref)

    def block(b, j):
        q_at = span(j, rows)
        dq_ref[...] = part_ref[j].astype(jnp.float32)

        def spread(start, size):
            picks, real = pick(list_ref, b, start, size)
            n = size * TILE
            load_tiles(kv_ref, k_ref, v_ref, picks)
            level = fin_ref[j, 0:1]
            delta = fin_ref[j, 1:2]
            x = dot(k_ref[:n], q_ref[q_at, :], NT) * scale
            dp = dot(v_ref[:n], do_ref[q_at, :], NT)
            for i in range(size):
                xi = mask_diagonal(x[part(i)], start == 0, group) if i == 0 else x[part(i)]
                p = jnp.exp2(xi - jnp.where(real[i], level, HIGH))
                p_ref[part(i)] = p.astype(jnp.bfloat16)
                ds_ref[part(i)] = (p * (dp[part(i)] - delta)).astype(jnp.bfloat16)
            add_grads(acc_ref, picks, dot(ds_ref[:n], q_ref[q_at, :]), dot(p_ref[:n], do_ref[q_at, :]))
            dq_ref[...] += dot(k_ref[:n], ds_ref[:n], TN)

        in_parts(list_ref[b, SEL], spread)
        out_ref[q_at, :] = (dq_ref[...] * inv_root).astype(out_ref.dtype).T

    each_block(block)
    leave_grads(inv_root, par_ref, acc_ref, keep_ref, send_ref)


def fill_reply(home_ref, mine_ref, reply_ref):
    cap = home_ref.shape[2]
    for i in range(home_ref.shape[0] * cap):
        t = jnp.maximum(home_ref[i // cap, 0, i % cap], 0)
        reply_ref[i * TILE : (i + 1) * TILE] = mine_ref[tile_rows(t), :]


def join_grads(home_ref, keep_ref, other_ref, came_ref, out_ref, acc_ref):
    cap = home_ref.shape[2]
    acc_ref[...] = keep_ref[...] + other_ref[...]
    for i in range(home_ref.shape[0] * cap):
        t = home_ref[i // cap, 0, i % cap]

        @pl.when(t >= 0)
        def _():
            acc_ref[tile_rows(t), :] += came_ref[i * TILE : (i + 1) * TILE].astype(jnp.float32)

    out_ref[...] = acc_ref[...].astype(out_ref.dtype)


def plan(blocks, me_ref, sel_ref, ask_ref, own_ref, far_ref):
    shards = ask_ref.shape[0]
    tiles = shards * blocks
    f32, bf16 = jnp.float32, jnp.bfloat16
    me = me_ref[0]
    sel = sel_ref[...]
    rows = sel.shape[0]
    tile = lax.broadcasted_iota(jnp.int32, (rows, tiles), 1)
    named = sel[:, 0:1] == tile
    for s in range(1, SEL):
        named = named | (sel[:, s : s + 1] == tile)
    is_own = tile // blocks == me
    own = jnp.where(named & is_own, 1.0, 0.0)
    far = jnp.where(named & jnp.logical_not(is_own), 1.0, 0.0)
    wanted = jnp.max(far, axis=0, keepdims=True)

    a = lax.broadcasted_iota(jnp.int32, (tiles, tiles), 0)
    b = lax.broadcasted_iota(jnp.int32, (tiles, tiles), 1)
    lower = jnp.where(a < b, 1.0, 0.0).astype(bf16)
    higher = jnp.where(a > b, 1.0, 0.0).astype(bf16)
    same = jnp.where((a < b) & (a // blocks == b // blocks), 1.0, 0.0).astype(bf16)
    own_place = dot(own.astype(bf16), higher)
    far_place = dot(far.astype(bf16), lower)
    rank = dot(jnp.broadcast_to(wanted, (rows, tiles)).astype(bf16), same)

    local = (tile % blocks).astype(f32)
    far_index = (tile // blocks * CAP).astype(f32) + rank
    column = lax.broadcasted_iota(jnp.int32, (rows, 128), 1)

    def packed(flags, place, values, most):
        out = jnp.where(column == SEL, jnp.sum(flags, axis=1, keepdims=True), 0.0)
        for p in range(most):
            here = jnp.sum(jnp.where(place == p, flags * values, 0.0), axis=1, keepdims=True)
            out = jnp.where(column == p, here, out)
        return out.astype(jnp.int32)[:, : SEL + 1]

    own_ref[...] = packed(own, own_place, local, SEL)
    far_ref[...] = packed(far, far_place, far_index, FAR_SIZES[-1])

    spot = lax.broadcasted_iota(jnp.int32, (rows, tiles), 0).astype(f32)
    asked = jnp.where((rank == spot) & (wanted > 0.0), local + 1.0, 0.0).astype(bf16)
    shard = lax.broadcasted_iota(jnp.int32, (shards, tiles), 0)
    owned = lax.broadcasted_iota(jnp.int32, (shards, tiles), 1) // blocks == shard
    asked = dot(jnp.where(owned, 1.0, 0.0).astype(bf16), asked, NT).astype(jnp.int32) - 1
    for e in range(shards):
        ask_ref[e] = asked[e : e + 1, :CAP]


def whole(shape):
    return pl.BlockSpec(shape, lambda b, *_: (0,) * len(shape), pipeline_mode=pl.Buffered(1))


def on_device(queries, keyvals, selected, d_out):
    tok_rows, heads, dim = queries.shape
    blocks = tok_rows // TILE
    shards = lax.axis_size("seq")
    me = lax.axis_index("seq")
    par = (lax.axis_index("head") % 2).astype(jnp.int32).reshape(1)
    inv_root = dim**-0.5
    scale = inv_root / math.log(2.0)
    rows = TILE * heads
    far = shards * CAP
    f32 = jnp.float32

    mine = keyvals[:, 0, :]
    theirs = swap_pair(mine)
    still = keep_in_hbm(mine)

    in_smem = pl.BlockSpec(memory_space=pltpu.SMEM)
    in_vmem = pl.BlockSpec(memory_space=pltpu.VMEM)
    asked, own_list, far_list = pl.pallas_call(
        functools.partial(plan, blocks),
        out_shape=(
            jax.ShapeDtypeStruct((shards, 1, CAP), jnp.int32),
            jax.ShapeDtypeStruct((blocks, SEL + 1), jnp.int32),
            jax.ShapeDtypeStruct((blocks, SEL + 1), jnp.int32),
        ),
        in_specs=[in_smem, in_vmem],
        out_specs=(in_vmem, in_vmem, in_vmem),
        compiler_params=pltpu.CompilerParams(vmem_limit_bytes=SMALL_LIMIT),
        name="plan",
    )(me.astype(jnp.int32).reshape(1), keep_in_hbm(selected))
    home = lax.all_to_all(asked, "seq", split_axis=0, concat_axis=0, tiled=True)
    home, theirs = lax.optimization_barrier((home, theirs))
    theirs = keep_in_hbm(theirs)
    reply = pl.pallas_call(
        fill_reply,
        out_shape=jax.ShapeDtypeStruct((far * TILE, dim), jnp.bfloat16),
        in_specs=[in_smem, in_vmem],
        out_specs=in_vmem,
        compiler_params=pltpu.CompilerParams(vmem_limit_bytes=SMALL_LIMIT),
        name="fill_reply",
    )(home, still)
    far_mine = lax.all_to_all(reply, "seq", split_axis=0, concat_axis=0, tiled=True)

    q2 = keep_in_hbm(queries.reshape(blocks * rows, dim))
    do2 = keep_in_hbm(d_out.reshape(blocks * rows, dim))
    blk = pl.BlockSpec((STEP * rows, dim), lambda b, *_: (b, 0))
    stat = pl.BlockSpec((STEP, 8, rows), lambda b, *_: (b, 0, 0))
    part_dq = pl.BlockSpec((STEP, dim, rows), lambda b, *_: (b, 0, 0))
    params = pltpu.CompilerParams(
        dimension_semantics=("arbitrary",), vmem_limit_bytes=VMEM_LIMIT
    )
    one = 2 * rows * TILE * dim
    bf16 = jnp.bfloat16
    own_rows, far_rows = (tok_rows, dim), (far * TILE, dim)
    some_keys = [pltpu.VMEM((WIDE * TILE, dim), bf16)] * 2
    some_probs = [pltpu.VMEM((WIDE * TILE, rows), bf16)] * 2

    stats = pl.pallas_call(
        functools.partial(own_stats, scale, heads),
        out_shape=jax.ShapeDtypeStruct((blocks, 8, rows), f32),
        grid_spec=pltpu.PrefetchScalarGridSpec(
            num_scalar_prefetch=2,
            grid=(blocks // STEP,),
            in_specs=[blk, blk, whole(own_rows), whole(own_rows)],
            out_specs=stat,
            scratch_shapes=[pltpu.VMEM((2,) + own_rows, bf16)] + some_keys + [pltpu.VMEM((STEP, 3, 8, rows), f32)],
        ),
        compiler_params=params,
        cost_estimate=pl.CostEstimate(
            flops=2 * one * blocks * 8, bytes_accessed=2 * tok_rows * heads * dim * 2, transcendentals=0
        ),
        name="own_stats",
    )(own_list, par, q2, do2, still, theirs)

    far_mine, stats = lax.optimization_barrier((far_mine, stats))
    far_theirs = swap_pair(far_mine)

    final, dq_part, far_keep, far_send = pl.pallas_call(
        functools.partial(far_grads, scale, inv_root),
        out_shape=(
            pltpu.HBM((blocks, 8, rows), f32),
            pltpu.HBM((blocks, dim, rows), f32),
            jax.ShapeDtypeStruct(far_rows, f32),
            jax.ShapeDtypeStruct(far_rows, bf16),
        ),
        grid_spec=pltpu.PrefetchScalarGridSpec(
            num_scalar_prefetch=2,
            grid=(blocks // STEP,),
            in_specs=[stat, blk, blk, whole(far_rows), whole(far_rows)],
            out_specs=(stat, part_dq, whole(far_rows), whole(far_rows)),
            scratch_shapes=[
                pltpu.VMEM((2,) + far_rows, bf16),
                pltpu.VMEM((2,) + far_rows, f32),
                pltpu.VMEM((STEP, WIDE * TILE, rows), f32),
                pltpu.VMEM((STEP, WIDE * TILE, rows), f32),
                pltpu.VMEM((STEP, 3, 8, rows), f32),
            ]
            + some_keys
            + some_probs,
        ),
        compiler_params=params,
        cost_estimate=pl.CostEstimate(
            flops=5 * one * blocks * 6, bytes_accessed=4 * tok_rows * heads * dim * 2, transcendentals=0
        ),
        name="far_grads",
    )(far_list, par, stats, q2, do2, far_mine, far_theirs)

    back = (far_keep + swap_pair(far_send).astype(f32)).astype(bf16)
    came = lax.all_to_all(back, "seq", split_axis=0, concat_axis=0, tiled=True)

    grad_q, own_keep, own_send = pl.pallas_call(
        functools.partial(own_grads, scale, inv_root, heads),
        out_shape=(
            jax.ShapeDtypeStruct((blocks * rows, dim), bf16),
            jax.ShapeDtypeStruct(own_rows, f32),
            jax.ShapeDtypeStruct(own_rows, f32),
        ),
        grid_spec=pltpu.PrefetchScalarGridSpec(
            num_scalar_prefetch=2,
            grid=(blocks // STEP,),
            in_specs=[stat, part_dq, blk, blk, whole(own_rows), whole(own_rows)],
            out_specs=(blk, whole(own_rows), whole(own_rows)),
            scratch_shapes=[
                pltpu.VMEM((2,) + own_rows, bf16),
                pltpu.VMEM((2,) + own_rows, f32),
                pltpu.VMEM((dim, rows), f32),
            ]
            + some_keys
            + some_probs,
        ),
        compiler_params=params,
        cost_estimate=pl.CostEstimate(
            flops=5 * one * blocks * 8, bytes_accessed=5 * tok_rows * heads * dim * 2, transcendentals=0
        ),
        name="own_grads",
    )(own_list, par, keep_in_hbm(final), keep_in_hbm(dq_part), q2, do2, still, theirs)

    other = swap_pair(own_send)
    grad_kv = pl.pallas_call(
        join_grads,
        out_shape=jax.ShapeDtypeStruct(own_rows, bf16),
        in_specs=[in_smem, in_vmem, in_vmem, in_vmem],
        out_specs=in_vmem,
        scratch_shapes=[pltpu.VMEM(own_rows, f32)],
        compiler_params=pltpu.CompilerParams(vmem_limit_bytes=SMALL_LIMIT),
        name="join_grads",
    )(home, own_keep, other, came)
    return (grad_q.reshape(tok_rows, heads, dim), grad_kv.reshape(tok_rows, 1, dim))


def solution(mesh):
    in_specs = (
        P("seq", "head", None),
        P("seq", "head", None),
        P("seq", None),
        P("seq", "head", None),
    )
    out_specs = (P("seq", "head", None), P("seq", "head", None))
    return jax.shard_map(
        on_device, mesh=mesh, in_specs=in_specs, out_specs=out_specs, check_vma=False
    )
```

```python
import functools
import math

import jax
import jax.numpy as jnp
from jax import lax
from jax.experimental import pallas as pl
from jax.experimental.pallas import tpu as pltpu
from jax.sharding import PartitionSpec as P

TILE = 64
SEL = 16
CAP = 3
WIDE = 8
OWN_SIZES = (2, 4, 6)
FAR_SIZES = (4, 7, 8)
VMEM_LIMIT = 40 * 1024 * 1024
SMALL_LIMIT = 8 * 1024 * 1024
STEP = 4
LOW = -1e30
HIGH = 1e30
TOO_LARGE = 2.0**64
NT = (((1,), (1,)), ((), ()))
TN = (((0,), (0,)), ((), ()))


def swap_pair(block):
    count = lax.axis_size("head")
    return lax.ppermute(block, "head", [(h, h ^ 1) for h in range(count)])


def keep_in_hbm(array):
    return pltpu.with_memory_space_constraint(array, pltpu.HBM)


def tile_rows(index):
    return pl.ds(pl.multiple_of(index * TILE, TILE), TILE)


def span(index, size):
    return pl.ds(pl.multiple_of(index * size, size), size)


def dot(a, b, dims=(((1,), (0,)), ((), ()))):
    return lax.dot_general(a, b, dims, preferred_element_type=jnp.float32)


def fold(x, op):
    parts = [x[8 * i : 8 * i + 8] for i in range(TILE // 8)]
    while len(parts) > 1:
        parts = [op(parts[i], parts[i + 1]) for i in range(0, len(parts), 2)]
    return parts[0]


def places(rows, group):
    key = lax.broadcasted_iota(jnp.int32, (TILE, rows), 0)
    query = lax.broadcasted_iota(jnp.int32, (TILE, rows), 1) // group
    return key, query


def mask_diagonal(x, is_first, group):
    key, query = places(x.shape[1], group)
    return jnp.where((key <= query) | jnp.logical_not(is_first), x, LOW)


def pick_diagonal(x, group):
    key, query = places(x.shape[1], group)
    return jnp.sum(fold(jnp.where(key == query, x, 0.0), jnp.add), axis=0, keepdims=True)


def lay_halves(par_ref, mine_ref, theirs_ref, kv_ref):
    par = par_ref[0]
    kv_ref[par] = mine_ref[...]
    kv_ref[1 - par] = theirs_ref[...]


def each_block(body):
    def run(j, _):
        body(pl.program_id(0) * STEP + j, j)
        return 0

    lax.fori_loop(0, STEP, run, 0)


def pick(list_ref, b, start, size):
    count = list_ref[b, SEL]
    return (
        [list_ref[b, start + i] for i in range(size)],
        [start + i < count for i in range(size)],
    )


def part(i):
    return slice(i * TILE, (i + 1) * TILE)


def load_tiles(kv_ref, k_ref, v_ref, picks):
    for i, t in enumerate(picks):
        k_ref[part(i)] = kv_ref[0, tile_rows(t), :]
        v_ref[part(i)] = kv_ref[1, tile_rows(t), :]


def by_size(left, sizes, run):
    for low, size in zip((0,) + sizes[:-1], sizes, strict=True):

        @pl.when((left > low) & (left <= size))
        def _():
            run(size)


def in_parts(count, run):
    wide = (count + 1) // WIDE

    def full(c, _):
        run(c * WIDE, WIDE)
        return 0

    lax.fori_loop(0, wide, full, 0)
    by_size(count - wide * WIDE, OWN_SIZES, lambda size: run(wide * WIDE, size))


def sum_up(x):
    return jnp.sum(x, axis=0, keepdims=True)


def own_stats(
    scale, group, list_ref, par_ref, q_ref, do_ref, mine_ref, theirs_ref, st_ref,
    kv_ref, k_ref, v_ref, sum_ref,
):
    rows = q_ref.shape[0] // STEP

    @pl.when(pl.program_id(0) == 0)
    def _():
        lay_halves(par_ref, mine_ref, theirs_ref, kv_ref)

    def block(b, j, again=False):
        count = list_ref[b, SEL]
        q_at = span(j, rows)
        sums = sum_ref.at[j]

        def scores(start, size):
            picks, real = pick(list_ref, b, start, size)
            load_tiles(kv_ref, k_ref, v_ref, picks)
            return dot(k_ref[: size * TILE], q_ref[q_at, :], NT) * scale, real

        def run(start, size):
            x, real = scores(start, size)
            dp = dot(v_ref[: size * TILE], do_ref[q_at, :], NT)
            base = sums[0]
            if not again:
                base = jnp.where(start == 0, pick_diagonal(x[part(0)], group), base)
                sums[0] = base
            base = base[0:1]
            total, dotted = sums[1], sums[2]
            for i in range(size):
                xi = mask_diagonal(x[part(i)], start == 0, group) if i == 0 else x[part(i)]
                e = jnp.exp2(xi - jnp.where(real[i], base, HIGH))
                total = total + fold(e, jnp.add)
                dotted = dotted + fold(e * dp[part(i)], jnp.add)
            sums[1] = total
            sums[2] = dotted

        if not again:
            sums[...] = jnp.zeros_like(sums)
            in_parts(count, run)
            return

        size = OWN_SIZES[0]
        sums[0] = jnp.full(sums.shape[1:], LOW, jnp.float32)

        def look(c, _):
            x, real = scores(c * size, size)
            top = sums[0]
            for i in range(size):
                xi = mask_diagonal(x[part(i)], c == 0, group) if i == 0 else x[part(i)]
                top = jnp.maximum(top, jnp.where(real[i], fold(xi, jnp.maximum), LOW))
            sums[0] = top
            return 0

        def anew(c, _):
            run(c * size, size)
            return 0

        lax.fori_loop(0, pl.cdiv(count, size), look, 0)
        sums[0] = jnp.broadcast_to(jnp.max(sums[0], axis=0, keepdims=True), sums.shape[1:])
        sums[1] = jnp.zeros(sums.shape[1:], jnp.float32)
        sums[2] = jnp.zeros(sums.shape[1:], jnp.float32)
        lax.fori_loop(0, pl.cdiv(count, size), anew, 0)

    each_block(block)

    @pl.when(jnp.max(sum_ref[:, 1]) > TOO_LARGE)
    def _():
        each_block(functools.partial(block, again=True))

    for j in range(STEP):
        st_ref[j, 0:1] = sum_ref[j, 0, 0:1]
        st_ref[j, 1:2] = sum_up(sum_ref[j, 1])
        st_ref[j, 2:3] = sum_up(sum_ref[j, 2])


def add_grads(acc_ref, picks, gk, gv):
    for i, t in enumerate(picks):
        acc_ref[0, tile_rows(t), :] += gk[part(i)]
        acc_ref[1, tile_rows(t), :] += gv[part(i)]


def leave_grads(inv_root, par_ref, acc_ref, keep_ref, send_ref):
    @pl.when(pl.program_id(0) == pl.num_programs(0) - 1)
    def _():
        par = par_ref[0]
        keep = acc_ref[par] * jnp.where(par == 0, inv_root, 1.0)
        send = acc_ref[1 - par] * jnp.where(par == 0, 1.0, inv_root)
        keep_ref[...] = keep.astype(keep_ref.dtype)
        send_ref[...] = send.astype(send_ref.dtype)


def far_grads(
    scale, inv_root, list_ref, par_ref, st_ref, q_ref, do_ref, mine_ref, theirs_ref,
    fin_ref, dq_ref, keep_ref, send_ref,
    kv_ref, acc_ref, e_ref, dp_ref, sum_ref, k_ref, v_ref, p_ref, ds_ref,
):
    rows = q_ref.shape[0] // STEP

    @pl.when(pl.program_id(0) == 0)
    def _():
        lay_halves(par_ref, mine_ref, theirs_ref, kv_ref)
        acc_ref[...] = jnp.zeros_like(acc_ref)

    def begin(j, base):
        fade = jnp.exp2(st_ref[j, 0:1] - base)
        at_top = lax.broadcasted_iota(jnp.int32, sum_ref.shape[2:], 0) == 0
        sum_ref[j, 0] = jnp.broadcast_to(base, sum_ref.shape[2:])
        sum_ref[j, 1] = jnp.where(at_top, st_ref[j, 1:2] * fade, 0.0)
        sum_ref[j, 2] = jnp.where(at_top, st_ref[j, 2:3] * fade, 0.0)

    def scores(b, j, half, start, size):
        picks, real = pick(list_ref, b, start, size)
        load_tiles(kv_ref, k_ref.at[half], v_ref.at[half], picks)
        return dot(k_ref[half, : size * TILE], q_ref[span(j, rows), :], NT) * scale, real

    def read(b, j, half, start, size):
        x, real = scores(b, j, half, start, size)
        dp = dot(v_ref[half, : size * TILE], do_ref[span(j, rows), :], NT)
        base, total, dotted = sum_ref[j, 0, 0:1], sum_ref[j, 1], sum_ref[j, 2]
        for i in range(size):
            to = tile_rows(start + i)
            e = jnp.exp2(x[part(i)] - jnp.where(real[i], base, HIGH))
            e_ref[j, to, :] = e
            dp_ref[j, to, :] = dp[part(i)]
            total = total + fold(e, jnp.add)
            dotted = dotted + fold(e * dp[part(i)], jnp.add)
        sum_ref[j, 1] = total
        sum_ref[j, 2] = dotted

    def anew(b, j):
        count = list_ref[b, SEL]
        size = FAR_SIZES[0]
        sum_ref[j, 0] = jnp.broadcast_to(st_ref[j, 0:1], sum_ref.shape[2:])

        def look(c, _):
            x, real = scores(b, j, 0, c * size, size)
            top = sum_ref[j, 0]
            for i in range(size):
                top = jnp.maximum(top, jnp.where(real[i], fold(x[part(i)], jnp.maximum), LOW))
            sum_ref[j, 0] = top
            return 0

        def once_more(c, _):
            read(b, j, 0, c * size, size)
            return 0

        lax.fori_loop(0, pl.cdiv(count, size), look, 0)
        begin(j, jnp.max(sum_ref[j, 0], axis=0, keepdims=True))
        lax.fori_loop(0, pl.cdiv(count, size), once_more, 0)

    def finish(j):
        total, dotted = sum_up(sum_ref[j, 1]), sum_up(sum_ref[j, 2])
        delta = dotted / total
        fin_ref[j, 0:1] = sum_ref[j, 0, 0:1] + jnp.log2(total)
        fin_ref[j, 1:2] = delta
        fin_ref[j, 2:3] = 1.0 / total

    def spread(b, j, half, size):
        picks, _ = pick(list_ref, b, 0, size)
        delta, ratio = fin_ref[j, 1:2], fin_ref[j, 2:3]
        n = size * TILE
        q_at = span(j, rows)
        for i, t in enumerate(picks):
            k_ref[half, part(i)] = kv_ref[0, tile_rows(t), :]
            p = e_ref[j, part(i)] * ratio
            p_ref[half, part(i)] = p.astype(jnp.bfloat16)
            ds_ref[half, part(i)] = (p * (dp_ref[j, part(i)] - delta)).astype(jnp.bfloat16)
        ds = ds_ref[half, :n]
        add_grads(acc_ref, picks, dot(ds, q_ref[q_at, :]), dot(p_ref[half, :n], do_ref[q_at, :]))
        dq_ref[j] = dot(k_ref[half, :n], ds, TN)

    def each_pair(body):
        def run(i, _):
            places = [2 * i, 2 * i + 1]
            pair = [(pl.program_id(0) * STEP + j, j) for j in places]
            body(pair, jnp.maximum(list_ref[pair[0][0], SEL], list_ref[pair[1][0], SEL]))
            return 0

        lax.fori_loop(0, STEP // 2, run, 0)

    def first(pair, count):
        for _, j in pair:
            begin(j, st_ref[j, 0:1])

        def both(size):
            for half, (b, j) in enumerate(pair):
                read(b, j, half, 0, size)

        by_size(count, FAR_SIZES, both)

    def second(pair, count):
        for _, j in pair:
            finish(j)

        @pl.when(count == 0)
        def _():
            for _, j in pair:
                dq_ref[j] = jnp.zeros(dq_ref.shape[1:], dq_ref.dtype)

        def both(size):
            for half, (b, j) in enumerate(pair):
                spread(b, j, half, size)

        by_size(count, FAR_SIZES, both)

    each_pair(first)

    @pl.when(jnp.max(sum_ref[:, 1]) > TOO_LARGE)
    def _():
        each_block(anew)

    each_pair(second)
    leave_grads(inv_root, par_ref, acc_ref, keep_ref, send_ref)


def own_grads(
    scale, inv_root, group, list_ref, par_ref, fin_ref, part_ref, q_ref, do_ref, mine_ref, theirs_ref,
    out_ref, keep_ref, send_ref, kv_ref, acc_ref, dq_ref, k_ref, v_ref, p_ref, ds_ref,
):
    rows = q_ref.shape[0] // STEP

    @pl.when(pl.program_id(0) == 0)
    def _():
        lay_halves(par_ref, mine_ref, theirs_ref, kv_ref)
        acc_ref[...] = jnp.zeros_like(acc_ref)

    def write(j):
        out_ref[span(j, rows), :] = (dq_ref[j] * inv_root).astype(out_ref.dtype).T

    def block(b, j):
        q_at = span(j, rows)
        dq_ref[j] = part_ref[j]

        def spread(start, size):
            picks, real = pick(list_ref, b, start, size)
            n = size * TILE
            load_tiles(kv_ref, k_ref, v_ref, picks)
            level = fin_ref[j, 0:1]
            delta = fin_ref[j, 1:2]
            x = dot(k_ref[:n], q_ref[q_at, :], NT) * scale
            dp = dot(v_ref[:n], do_ref[q_at, :], NT)
            for i in range(size):
                xi = mask_diagonal(x[part(i)], start == 0, group) if i == 0 else x[part(i)]
                p = jnp.exp2(xi - jnp.where(real[i], level, HIGH))
                p_ref[part(i)] = p.astype(jnp.bfloat16)
                ds_ref[part(i)] = (p * (dp[part(i)] - delta)).astype(jnp.bfloat16)
            write(jnp.maximum(j - 1, 0))
            add_grads(acc_ref, picks, dot(ds_ref[:n], q_ref[q_at, :]), dot(p_ref[:n], do_ref[q_at, :]))
            dq_ref[j] += dot(k_ref[:n], ds_ref[:n], TN)

        in_parts(list_ref[b, SEL], spread)

    each_block(block)
    write(STEP - 1)
    leave_grads(inv_root, par_ref, acc_ref, keep_ref, send_ref)


def fill_reply(home_ref, mine_ref, reply_ref):
    cap = home_ref.shape[2]
    for i in range(home_ref.shape[0] * cap):
        t = jnp.maximum(home_ref[i // cap, 0, i % cap], 0)
        reply_ref[i * TILE : (i + 1) * TILE] = mine_ref[tile_rows(t), :]


def join_grads(home_ref, keep_ref, other_ref, came_ref, out_ref, acc_ref):
    cap = home_ref.shape[2]
    acc_ref[...] = keep_ref[...] + other_ref[...]
    for i in range(home_ref.shape[0] * cap):
        t = home_ref[i // cap, 0, i % cap]

        @pl.when(t >= 0)
        def _():
            acc_ref[tile_rows(t), :] += came_ref[i * TILE : (i + 1) * TILE].astype(jnp.float32)

    out_ref[...] = acc_ref[...].astype(out_ref.dtype)


def plan(blocks, me_ref, sel_ref, ask_ref, own_ref, far_ref):
    shards = ask_ref.shape[0]
    tiles = shards * blocks
    f32, bf16 = jnp.float32, jnp.bfloat16
    me = me_ref[0]
    sel = sel_ref[...]
    rows = sel.shape[0]
    tile = lax.broadcasted_iota(jnp.int32, (rows, tiles), 1)
    named = sel[:, 0:1] == tile
    for s in range(1, SEL):
        named = named | (sel[:, s : s + 1] == tile)
    is_own = tile // blocks == me
    own = jnp.where(named & is_own, 1.0, 0.0)
    far = jnp.where(named & jnp.logical_not(is_own), 1.0, 0.0)
    wanted = jnp.max(far, axis=0, keepdims=True)

    a = lax.broadcasted_iota(jnp.int32, (tiles, tiles), 0)
    b = lax.broadcasted_iota(jnp.int32, (tiles, tiles), 1)
    lower = jnp.where(a < b, 1.0, 0.0).astype(bf16)
    higher = jnp.where(a > b, 1.0, 0.0).astype(bf16)
    same = jnp.where((a < b) & (a // blocks == b // blocks), 1.0, 0.0).astype(bf16)
    own_place = dot(own.astype(bf16), higher)
    far_place = dot(far.astype(bf16), lower)
    rank = dot(jnp.broadcast_to(wanted, (rows, tiles)).astype(bf16), same)

    local = (tile % blocks).astype(f32)
    far_index = (tile // blocks * CAP).astype(f32) + rank
    column = lax.broadcasted_iota(jnp.int32, (rows, 128), 1)

    def packed(flags, place, values, most):
        out = jnp.where(column == SEL, jnp.sum(flags, axis=1, keepdims=True), 0.0)
        for p in range(most):
            here = jnp.sum(jnp.where(place == p, flags * values, 0.0), axis=1, keepdims=True)
            out = jnp.where(column == p, here, out)
        return out.astype(jnp.int32)[:, : SEL + 1]

    own_ref[...] = packed(own, own_place, local, SEL)
    far_ref[...] = packed(far, far_place, far_index, FAR_SIZES[-1])

    spot = lax.broadcasted_iota(jnp.int32, (rows, tiles), 0).astype(f32)
    asked = jnp.where((rank == spot) & (wanted > 0.0), local + 1.0, 0.0).astype(bf16)
    shard = lax.broadcasted_iota(jnp.int32, (shards, tiles), 0)
    owned = lax.broadcasted_iota(jnp.int32, (shards, tiles), 1) // blocks == shard
    asked = dot(jnp.where(owned, 1.0, 0.0).astype(bf16), asked, NT).astype(jnp.int32) - 1
    for e in range(shards):
        ask_ref[e] = asked[e : e + 1, :CAP]


def whole(shape):
    return pl.BlockSpec(shape, lambda b, *_: (0,) * len(shape), pipeline_mode=pl.Buffered(1))


def on_device(queries, keyvals, selected, d_out):
    tok_rows, heads, dim = queries.shape
    blocks = tok_rows // TILE
    shards = lax.axis_size("seq")
    me = lax.axis_index("seq")
    par = (lax.axis_index("head") % 2).astype(jnp.int32).reshape(1)
    inv_root = dim**-0.5
    scale = inv_root / math.log(2.0)
    rows = TILE * heads
    far = shards * CAP
    f32 = jnp.float32

    mine = keyvals[:, 0, :]
    theirs = swap_pair(mine)
    still = keep_in_hbm(mine)

    in_smem = pl.BlockSpec(memory_space=pltpu.SMEM)
    in_vmem = pl.BlockSpec(memory_space=pltpu.VMEM)
    asked, own_list, far_list = pl.pallas_call(
        functools.partial(plan, blocks),
        out_shape=(
            jax.ShapeDtypeStruct((shards, 1, CAP), jnp.int32),
            jax.ShapeDtypeStruct((blocks, SEL + 1), jnp.int32),
            jax.ShapeDtypeStruct((blocks, SEL + 1), jnp.int32),
        ),
        in_specs=[in_smem, in_vmem],
        out_specs=(in_vmem, in_vmem, in_vmem),
        compiler_params=pltpu.CompilerParams(vmem_limit_bytes=SMALL_LIMIT),
        name="plan",
    )(me.astype(jnp.int32).reshape(1), keep_in_hbm(selected))
    home = lax.all_to_all(asked, "seq", split_axis=0, concat_axis=0, tiled=True)
    home, theirs = lax.optimization_barrier((home, theirs))
    theirs = keep_in_hbm(theirs)
    reply = pl.pallas_call(
        fill_reply,
        out_shape=jax.ShapeDtypeStruct((far * TILE, dim), jnp.bfloat16),
        in_specs=[in_smem, in_vmem],
        out_specs=in_vmem,
        compiler_params=pltpu.CompilerParams(vmem_limit_bytes=SMALL_LIMIT),
        name="fill_reply",
    )(home, still)
    far_mine = lax.all_to_all(reply, "seq", split_axis=0, concat_axis=0, tiled=True)

    q2 = keep_in_hbm(queries.reshape(blocks * rows, dim))
    do2 = keep_in_hbm(d_out.reshape(blocks * rows, dim))
    blk = pl.BlockSpec((STEP * rows, dim), lambda b, *_: (b, 0))
    stat = pl.BlockSpec((STEP, 8, rows), lambda b, *_: (b, 0, 0))
    part_dq = pl.BlockSpec((STEP, dim, rows), lambda b, *_: (b, 0, 0))
    params = pltpu.CompilerParams(
        dimension_semantics=("arbitrary",), vmem_limit_bytes=VMEM_LIMIT
    )
    one = 2 * rows * TILE * dim
    bf16 = jnp.bfloat16
    own_rows, far_rows = (tok_rows, dim), (far * TILE, dim)
    some_keys = [pltpu.VMEM((WIDE * TILE, dim), bf16)] * 2
    some_probs = [pltpu.VMEM((WIDE * TILE, rows), bf16)] * 2

    stats = pl.pallas_call(
        functools.partial(own_stats, scale, heads),
        out_shape=jax.ShapeDtypeStruct((blocks, 8, rows), f32),
        grid_spec=pltpu.PrefetchScalarGridSpec(
            num_scalar_prefetch=2,
            grid=(blocks // STEP,),
            in_specs=[blk, blk, whole(own_rows), whole(own_rows)],
            out_specs=stat,
            scratch_shapes=[pltpu.VMEM((2,) + own_rows, bf16)] + some_keys + [pltpu.VMEM((STEP, 3, 8, rows), f32)],
        ),
        compiler_params=params,
        cost_estimate=pl.CostEstimate(
            flops=2 * one * blocks * 8, bytes_accessed=2 * tok_rows * heads * dim * 2, transcendentals=0
        ),
        name="own_stats",
    )(own_list, par, q2, do2, still, theirs)

    far_mine, stats = lax.optimization_barrier((far_mine, stats))
    far_theirs = swap_pair(far_mine)

    final, dq_part, far_keep, far_send = pl.pallas_call(
        functools.partial(far_grads, scale, inv_root),
        out_shape=(
            pltpu.HBM((blocks, 8, rows), f32),
            pltpu.HBM((blocks, dim, rows), f32),
            jax.ShapeDtypeStruct(far_rows, f32),
            jax.ShapeDtypeStruct(far_rows, bf16),
        ),
        grid_spec=pltpu.PrefetchScalarGridSpec(
            num_scalar_prefetch=2,
            grid=(blocks // STEP,),
            in_specs=[stat, blk, blk, whole(far_rows), whole(far_rows)],
            out_specs=(stat, part_dq, whole(far_rows), whole(far_rows)),
            scratch_shapes=[
                pltpu.VMEM((2,) + far_rows, bf16),
                pltpu.VMEM((2,) + far_rows, f32),
                pltpu.VMEM((STEP, WIDE * TILE, rows), f32),
                pltpu.VMEM((STEP, WIDE * TILE, rows), f32),
                pltpu.VMEM((STEP, 3, 8, rows), f32),
            ]
            + [pltpu.VMEM((2, WIDE * TILE, dim), bf16)] * 2
            + [pltpu.VMEM((2, WIDE * TILE, rows), bf16)] * 2,
        ),
        compiler_params=params,
        cost_estimate=pl.CostEstimate(
            flops=5 * one * blocks * 6, bytes_accessed=4 * tok_rows * heads * dim * 2, transcendentals=0
        ),
        name="far_grads",
    )(far_list, par, stats, q2, do2, far_mine, far_theirs)

    back = (far_keep + swap_pair(far_send).astype(f32)).astype(bf16)
    came = lax.all_to_all(back, "seq", split_axis=0, concat_axis=0, tiled=True)

    grad_q, own_keep, own_send = pl.pallas_call(
        functools.partial(own_grads, scale, inv_root, heads),
        out_shape=(
            jax.ShapeDtypeStruct((blocks * rows, dim), bf16),
            jax.ShapeDtypeStruct(own_rows, f32),
            jax.ShapeDtypeStruct(own_rows, f32),
        ),
        grid_spec=pltpu.PrefetchScalarGridSpec(
            num_scalar_prefetch=2,
            grid=(blocks // STEP,),
            in_specs=[stat, part_dq, blk, blk, whole(own_rows), whole(own_rows)],
            out_specs=(blk, whole(own_rows), whole(own_rows)),
            scratch_shapes=[
                pltpu.VMEM((2,) + own_rows, bf16),
                pltpu.VMEM((2,) + own_rows, f32),
                pltpu.VMEM((STEP, dim, rows), f32),
            ]
            + some_keys
            + some_probs,
        ),
        compiler_params=params,
        cost_estimate=pl.CostEstimate(
            flops=5 * one * blocks * 8, bytes_accessed=5 * tok_rows * heads * dim * 2, transcendentals=0
        ),
        name="own_grads",
    )(own_list, par, keep_in_hbm(final), keep_in_hbm(dq_part), q2, do2, still, theirs)

    other = swap_pair(own_send)
    grad_kv = pl.pallas_call(
        join_grads,
        out_shape=jax.ShapeDtypeStruct(own_rows, bf16),
        in_specs=[in_smem, in_vmem, in_vmem, in_vmem],
        out_specs=in_vmem,
        scratch_shapes=[pltpu.VMEM(own_rows, f32)],
        compiler_params=pltpu.CompilerParams(vmem_limit_bytes=SMALL_LIMIT),
        name="join_grads",
    )(home, own_keep, other, came)
    return (grad_q.reshape(tok_rows, heads, dim), grad_kv.reshape(tok_rows, 1, dim))


def solution(mesh):
    in_specs = (
        P("seq", "head", None),
        P("seq", "head", None),
        P("seq", None),
        P("seq", "head", None),
    )
    out_specs = (P("seq", "head", None), P("seq", "head", None))
    return jax.shard_map(
        on_device, mesh=mesh, in_specs=in_specs, out_specs=out_specs, check_vma=False
    )
```

```python
import functools
import math

import jax
import jax.numpy as jnp
from jax import lax
from jax.experimental import pallas as pl
from jax.experimental.pallas import tpu as pltpu
from jax.sharding import PartitionSpec as P

TILE = 64
SEL = 16
CAP = 3
WIDE = 8
OWN_SIZES = (2, 4, 5, 6, 7)
FAR_SIZES = (4, 7, 8)
VMEM_LIMIT = 40 * 1024 * 1024
SMALL_LIMIT = 8 * 1024 * 1024
STEP = 4
LOW = -1e30
HIGH = 1e30
TOO_LARGE = 2.0**64
NT = (((1,), (1,)), ((), ()))
TN = (((0,), (0,)), ((), ()))


def swap_pair(block):
    count = lax.axis_size("head")
    return lax.ppermute(block, "head", [(h, h ^ 1) for h in range(count)])


def keep_in_hbm(array):
    return pltpu.with_memory_space_constraint(array, pltpu.HBM)


def tile_rows(index):
    return pl.ds(pl.multiple_of(index * TILE, TILE), TILE)


def span(index, size):
    return pl.ds(pl.multiple_of(index * size, size), size)


def dot(a, b, dims=(((1,), (0,)), ((), ()))):
    return lax.dot_general(a, b, dims, preferred_element_type=jnp.float32)


def fold(x, op):
    parts = [x[8 * i : 8 * i + 8] for i in range(TILE // 8)]
    while len(parts) > 1:
        parts = [op(parts[i], parts[i + 1]) for i in range(0, len(parts), 2)]
    return parts[0]


def places(rows, group):
    key = lax.broadcasted_iota(jnp.int32, (TILE, rows), 0)
    query = lax.broadcasted_iota(jnp.int32, (TILE, rows), 1) // group
    return key, query


def mask_diagonal(x, is_first, group):
    key, query = places(x.shape[1], group)
    return jnp.where((key <= query) | jnp.logical_not(is_first), x, LOW)


def pick_diagonal(x, group):
    key, query = places(x.shape[1], group)
    return jnp.sum(fold(jnp.where(key == query, x, 0.0), jnp.add), axis=0, keepdims=True)


def lay_halves(par_ref, mine_ref, theirs_ref, kv_ref):
    par = par_ref[0]
    kv_ref[par] = mine_ref[...]
    kv_ref[1 - par] = theirs_ref[...]


def each_block(body):
    def run(j, _):
        body(pl.program_id(0) * STEP + j, j)
        return 0

    lax.fori_loop(0, STEP, run, 0)


def each_pair(list_ref, body):
    def run(i, _):
        pair = [(pl.program_id(0) * STEP + j, j) for j in (2 * i, 2 * i + 1)]
        body(i, pair, jnp.maximum(list_ref[pair[0][0], SEL], list_ref[pair[1][0], SEL]))
        return 0

    lax.fori_loop(0, STEP // 2, run, 0)


def pick(list_ref, b, start, size):
    count = list_ref[b, SEL]
    return (
        [list_ref[b, start + i] for i in range(size)],
        [start + i < count for i in range(size)],
    )


def part(i):
    return slice(i * TILE, (i + 1) * TILE)


def load_tiles(kv_ref, k_ref, v_ref, picks):
    for i, t in enumerate(picks):
        k_ref[part(i)] = kv_ref[0, tile_rows(t), :]
        v_ref[part(i)] = kv_ref[1, tile_rows(t), :]


def by_size(left, sizes, run):
    for low, size in zip((0,) + sizes[:-1], sizes, strict=True):

        @pl.when((left > low) & (left <= size))
        def _():
            run(size)


def in_parts(count, run):
    wide = count // WIDE

    def full(c, _):
        run(c * WIDE, WIDE)
        return 0

    lax.fori_loop(0, wide, full, 0)
    by_size(count - wide * WIDE, OWN_SIZES, lambda size: run(wide * WIDE, size))


def sum_up(x):
    return jnp.sum(x, axis=0, keepdims=True)


def own_stats(
    scale, group, list_ref, par_ref, q_ref, do_ref, mine_ref, theirs_ref, st_ref,
    kv_ref, k_ref, v_ref, sum_ref,
):
    rows = q_ref.shape[0] // STEP

    @pl.when(pl.program_id(0) == 0)
    def _():
        lay_halves(par_ref, mine_ref, theirs_ref, kv_ref)

    def scores(b, j, half, start, size):
        picks, real = pick(list_ref, b, start, size)
        load_tiles(kv_ref, k_ref.at[half], v_ref.at[half], picks)
        return dot(k_ref[half, : size * TILE], q_ref[span(j, rows), :], NT) * scale, real

    def run(b, j, half, start, size, fresh):
        x, real = scores(b, j, half, start, size)
        dp = dot(v_ref[half, : size * TILE], do_ref[span(j, rows), :], NT)
        base = sum_ref[j, 0]
        if fresh:
            base = jnp.where(start == 0, pick_diagonal(x[part(0)], group), base)
            sum_ref[j, 0] = base
        base = base[0:1]
        total, dotted = sum_ref[j, 1], sum_ref[j, 2]
        for i in range(size):
            xi = mask_diagonal(x[part(i)], start == 0, group) if i == 0 else x[part(i)]
            e = jnp.exp2(xi - jnp.where(real[i], base, HIGH))
            total = total + fold(e, jnp.add)
            dotted = dotted + fold(e * dp[part(i)], jnp.add)
        sum_ref[j, 1] = total
        sum_ref[j, 2] = dotted

    def first(_, pair, count):
        def both(start, size):
            for half, (b, j) in enumerate(pair):
                run(b, j, half, start, size, True)

        in_parts(count, both)

    def anew(b, j):
        count = list_ref[b, SEL]
        size = OWN_SIZES[0]
        clear = jnp.zeros(sum_ref.shape[2:], jnp.float32)
        sum_ref[j, 0] = clear + LOW

        def look(c, _):
            x, real = scores(b, j, 0, c * size, size)
            top = sum_ref[j, 0]
            for i in range(size):
                xi = mask_diagonal(x[part(i)], c == 0, group) if i == 0 else x[part(i)]
                top = jnp.maximum(top, jnp.where(real[i], fold(xi, jnp.maximum), LOW))
            sum_ref[j, 0] = top
            return 0

        def once_more(c, _):
            run(b, j, 0, c * size, size, False)
            return 0

        lax.fori_loop(0, pl.cdiv(count, size), look, 0)
        sum_ref[j, 0] = clear + jnp.max(sum_ref[j, 0], axis=0, keepdims=True)
        sum_ref[j, 1] = clear
        sum_ref[j, 2] = clear
        lax.fori_loop(0, pl.cdiv(count, size), once_more, 0)

    sum_ref[...] = jnp.zeros_like(sum_ref)
    each_pair(list_ref, first)

    @pl.when(jnp.max(sum_ref[:, 1]) > TOO_LARGE)
    def _():
        each_block(anew)

    for j in range(STEP):
        st_ref[j, 0:1] = sum_ref[j, 0, 0:1]
        st_ref[j, 1:2] = sum_up(sum_ref[j, 1])
        st_ref[j, 2:3] = sum_up(sum_ref[j, 2])


def add_grads(acc_ref, picks, gk, gv):
    for i, t in enumerate(picks):
        acc_ref[0, tile_rows(t), :] += gk[part(i)]
        acc_ref[1, tile_rows(t), :] += gv[part(i)]


def leave_grads(inv_root, par_ref, acc_ref, keep_ref, send_ref):
    @pl.when(pl.program_id(0) == pl.num_programs(0) - 1)
    def _():
        par = par_ref[0]
        keep = acc_ref[par] * jnp.where(par == 0, inv_root, 1.0)
        send = acc_ref[1 - par] * jnp.where(par == 0, 1.0, inv_root)
        keep_ref[...] = keep.astype(keep_ref.dtype)
        send_ref[...] = send.astype(send_ref.dtype)


def far_grads(
    scale, inv_root, list_ref, par_ref, st_ref, q_ref, do_ref, mine_ref, theirs_ref,
    fin_ref, dq_ref, keep_ref, send_ref,
    kv_ref, acc_ref, e_ref, dp_ref, sum_ref, k_ref, v_ref, p_ref, ds_ref,
):
    rows = q_ref.shape[0] // STEP

    @pl.when(pl.program_id(0) == 0)
    def _():
        lay_halves(par_ref, mine_ref, theirs_ref, kv_ref)
        acc_ref[...] = jnp.zeros_like(acc_ref)

    def begin(j, base):
        fade = jnp.exp2(st_ref[j, 0:1] - base)
        at_top = lax.broadcasted_iota(jnp.int32, sum_ref.shape[2:], 0) == 0
        sum_ref[j, 0] = jnp.broadcast_to(base, sum_ref.shape[2:])
        sum_ref[j, 1] = jnp.where(at_top, st_ref[j, 1:2] * fade, 0.0)
        sum_ref[j, 2] = jnp.where(at_top, st_ref[j, 2:3] * fade, 0.0)

    def scores(b, j, half, start, size):
        picks, real = pick(list_ref, b, start, size)
        load_tiles(kv_ref, k_ref.at[half], v_ref.at[half], picks)
        return dot(k_ref[half, : size * TILE], q_ref[span(j, rows), :], NT) * scale, real

    def read(b, j, half, start, size):
        x, real = scores(b, j, half, start, size)
        dp = dot(v_ref[half, : size * TILE], do_ref[span(j, rows), :], NT)
        base, total, dotted = sum_ref[j, 0, 0:1], sum_ref[j, 1], sum_ref[j, 2]
        for i in range(size):
            to = tile_rows(start + i)
            e = jnp.exp2(x[part(i)] - jnp.where(real[i], base, HIGH))
            e_ref[j, to, :] = e
            dp_ref[j, to, :] = dp[part(i)]
            total = total + fold(e, jnp.add)
            dotted = dotted + fold(e * dp[part(i)], jnp.add)
        sum_ref[j, 1] = total
        sum_ref[j, 2] = dotted

    def anew(b, j):
        count = list_ref[b, SEL]
        size = FAR_SIZES[0]
        sum_ref[j, 0] = jnp.broadcast_to(st_ref[j, 0:1], sum_ref.shape[2:])

        def look(c, _):
            x, real = scores(b, j, 0, c * size, size)
            top = sum_ref[j, 0]
            for i in range(size):
                top = jnp.maximum(top, jnp.where(real[i], fold(x[part(i)], jnp.maximum), LOW))
            sum_ref[j, 0] = top
            return 0

        def once_more(c, _):
            read(b, j, 0, c * size, size)
            return 0

        lax.fori_loop(0, pl.cdiv(count, size), look, 0)
        begin(j, jnp.max(sum_ref[j, 0], axis=0, keepdims=True))
        lax.fori_loop(0, pl.cdiv(count, size), once_more, 0)

    def finish(j):
        total, dotted = sum_up(sum_ref[j, 1]), sum_up(sum_ref[j, 2])
        delta = dotted / total
        fin_ref[j, 0:1] = sum_ref[j, 0, 0:1] + jnp.log2(total)
        fin_ref[j, 1:2] = delta
        fin_ref[j, 2:3] = 1.0 / total

    def spread(b, j, half, size):
        picks, _ = pick(list_ref, b, 0, size)
        delta, ratio = fin_ref[j, 1:2], fin_ref[j, 2:3]
        n = size * TILE
        q_at = span(j, rows)
        for i, t in enumerate(picks):
            k_ref[half, part(i)] = kv_ref[0, tile_rows(t), :]
            p = e_ref[j, part(i)] * ratio
            p_ref[half, part(i)] = p.astype(jnp.bfloat16)
            ds_ref[half, part(i)] = (p * (dp_ref[j, part(i)] - delta)).astype(jnp.bfloat16)
        ds = ds_ref[half, :n]
        add_grads(acc_ref, picks, dot(ds, q_ref[q_at, :]), dot(p_ref[half, :n], do_ref[q_at, :]))
        dq_ref[j] = dot(k_ref[half, :n], ds, TN)

    def first(_, pair, count):
        for _, j in pair:
            begin(j, st_ref[j, 0:1])

        def both(size):
            for half, (b, j) in enumerate(pair):
                read(b, j, half, 0, size)

        by_size(count, FAR_SIZES, both)

    def second(_, pair, count):
        for _, j in pair:
            finish(j)

        @pl.when(count == 0)
        def _():
            for _, j in pair:
                dq_ref[j] = jnp.zeros(dq_ref.shape[1:], dq_ref.dtype)

        def both(size):
            for half, (b, j) in enumerate(pair):
                spread(b, j, half, size)

        by_size(count, FAR_SIZES, both)

    each_pair(list_ref, first)

    @pl.when(jnp.max(sum_ref[:, 1]) > TOO_LARGE)
    def _():
        each_block(anew)

    each_pair(list_ref, second)
    leave_grads(inv_root, par_ref, acc_ref, keep_ref, send_ref)


def own_grads(
    scale, inv_root, group, list_ref, par_ref, fin_ref, part_ref, q_ref, do_ref, mine_ref, theirs_ref,
    out_ref, keep_ref, send_ref, kv_ref, acc_ref, dq_ref, k_ref, v_ref, p_ref, ds_ref,
):
    rows = q_ref.shape[0] // STEP

    @pl.when(pl.program_id(0) == 0)
    def _():
        lay_halves(par_ref, mine_ref, theirs_ref, kv_ref)
        acc_ref[...] = jnp.zeros_like(acc_ref)

    def write(j):
        out_ref[span(j, rows), :] = (dq_ref[j] * inv_root).astype(out_ref.dtype).T

    def spread(b, j, half, start, size):
        q_at = span(j, rows)
        picks, real = pick(list_ref, b, start, size)
        n = size * TILE
        load_tiles(kv_ref, k_ref.at[half], v_ref.at[half], picks)
        level = fin_ref[j, 0:1]
        delta = fin_ref[j, 1:2]
        x = dot(k_ref[half, :n], q_ref[q_at, :], NT) * scale
        dp = dot(v_ref[half, :n], do_ref[q_at, :], NT)
        for i in range(size):
            xi = mask_diagonal(x[part(i)], start == 0, group) if i == 0 else x[part(i)]
            p = jnp.exp2(xi - jnp.where(real[i], level, HIGH))
            p_ref[half, part(i)] = p.astype(jnp.bfloat16)
            ds_ref[half, part(i)] = (p * (dp[part(i)] - delta)).astype(jnp.bfloat16)
        ds = ds_ref[half, :n]
        add_grads(acc_ref, picks, dot(ds, q_ref[q_at, :]), dot(p_ref[half, :n], do_ref[q_at, :]))
        dq_ref[j] += dot(k_ref[half, :n], ds, TN)

    def work(i, pair, count):
        for _, j in pair:
            dq_ref[j] = part_ref[j]
        before = 2 * jnp.maximum(i - 1, 0)

        def both(start, size):
            for half, (b, j) in enumerate(pair):
                spread(b, j, half, start, size)
                write(before + half)

        in_parts(count, both)

    each_pair(list_ref, work)
    write(STEP - 2)
    write(STEP - 1)
    leave_grads(inv_root, par_ref, acc_ref, keep_ref, send_ref)


def fill_reply(home_ref, mine_ref, reply_ref):
    cap = home_ref.shape[2]
    for i in range(home_ref.shape[0] * cap):
        t = jnp.maximum(home_ref[i // cap, 0, i % cap], 0)
        reply_ref[i * TILE : (i + 1) * TILE] = mine_ref[tile_rows(t), :]


def join_grads(home_ref, keep_ref, other_ref, came_ref, out_ref, acc_ref):
    cap = home_ref.shape[2]
    acc_ref[...] = keep_ref[...] + other_ref[...]
    for i in range(home_ref.shape[0] * cap):
        t = home_ref[i // cap, 0, i % cap]

        @pl.when(t >= 0)
        def _():
            acc_ref[tile_rows(t), :] += came_ref[i * TILE : (i + 1) * TILE].astype(jnp.float32)

    out_ref[...] = acc_ref[...].astype(out_ref.dtype)


def plan(blocks, me_ref, sel_ref, ask_ref, own_ref, far_ref):
    shards = ask_ref.shape[0]
    tiles = shards * blocks
    f32, bf16 = jnp.float32, jnp.bfloat16
    me = me_ref[0]
    sel = sel_ref[...]
    rows = sel.shape[0]
    tile = lax.broadcasted_iota(jnp.int32, (rows, tiles), 1)
    named = sel[:, 0:1] == tile
    for s in range(1, SEL):
        named = named | (sel[:, s : s + 1] == tile)
    is_own = (tile // blocks == me) & (
        (me > 0) | (tile >= CAP) | (tile == lax.broadcasted_iota(jnp.int32, tile.shape, 0))
    )
    own = jnp.where(named & is_own, 1.0, 0.0)
    far = jnp.where(named & jnp.logical_not(is_own), 1.0, 0.0)
    wanted = jnp.max(far, axis=0, keepdims=True)

    a = lax.broadcasted_iota(jnp.int32, (tiles, tiles), 0)
    b = lax.broadcasted_iota(jnp.int32, (tiles, tiles), 1)
    lower = jnp.where(a < b, 1.0, 0.0).astype(bf16)
    higher = jnp.where(a > b, 1.0, 0.0).astype(bf16)
    same = jnp.where((a < b) & (a // blocks == b // blocks), 1.0, 0.0).astype(bf16)
    own_place = dot(own.astype(bf16), higher)
    far_place = dot(far.astype(bf16), lower)
    rank = dot(jnp.broadcast_to(wanted, (rows, tiles)).astype(bf16), same)

    local = (tile % blocks).astype(f32)
    far_index = (tile // blocks * CAP).astype(f32) + rank
    column = lax.broadcasted_iota(jnp.int32, (rows, 128), 1)

    def packed(flags, place, values, most):
        out = jnp.where(column == SEL, jnp.sum(flags, axis=1, keepdims=True), 0.0)
        for p in range(most):
            here = jnp.sum(jnp.where(place == p, flags * values, 0.0), axis=1, keepdims=True)
            out = jnp.where(column == p, here, out)
        return out.astype(jnp.int32)[:, : SEL + 1]

    own_ref[...] = packed(own, own_place, local, SEL)
    far_ref[...] = packed(far, far_place, far_index, FAR_SIZES[-1])

    spot = lax.broadcasted_iota(jnp.int32, (rows, tiles), 0).astype(f32)
    asked = jnp.where((rank == spot) & (wanted > 0.0), local + 1.0, 0.0).astype(bf16)
    shard = lax.broadcasted_iota(jnp.int32, (shards, tiles), 0)
    owned = lax.broadcasted_iota(jnp.int32, (shards, tiles), 1) // blocks == shard
    asked = dot(jnp.where(owned, 1.0, 0.0).astype(bf16), asked, NT).astype(jnp.int32) - 1
    for e in range(shards):
        ask_ref[e] = asked[e : e + 1, :CAP]


def whole(shape):
    return pl.BlockSpec(shape, lambda b, *_: (0,) * len(shape), pipeline_mode=pl.Buffered(1))


def on_device(queries, keyvals, selected, d_out):
    tok_rows, heads, dim = queries.shape
    blocks = tok_rows // TILE
    shards = lax.axis_size("seq")
    me = lax.axis_index("seq")
    par = (lax.axis_index("head") % 2).astype(jnp.int32).reshape(1)
    inv_root = dim**-0.5
    scale = inv_root / math.log(2.0)
    rows = TILE * heads
    far = shards * CAP
    f32 = jnp.float32

    mine = keyvals[:, 0, :]
    theirs = swap_pair(mine)
    still = keep_in_hbm(mine)

    in_smem = pl.BlockSpec(memory_space=pltpu.SMEM)
    in_vmem = pl.BlockSpec(memory_space=pltpu.VMEM)
    asked, own_list, far_list = pl.pallas_call(
        functools.partial(plan, blocks),
        out_shape=(
            jax.ShapeDtypeStruct((shards, 1, CAP), jnp.int32),
            jax.ShapeDtypeStruct((blocks, SEL + 1), jnp.int32),
            jax.ShapeDtypeStruct((blocks, SEL + 1), jnp.int32),
        ),
        in_specs=[in_smem, in_vmem],
        out_specs=(in_vmem, in_vmem, in_vmem),
        compiler_params=pltpu.CompilerParams(vmem_limit_bytes=SMALL_LIMIT),
        name="plan",
    )(me.astype(jnp.int32).reshape(1), keep_in_hbm(selected))
    home = lax.all_to_all(asked, "seq", split_axis=0, concat_axis=0, tiled=True)
    home, theirs = lax.optimization_barrier((home, theirs))
    theirs = keep_in_hbm(theirs)
    reply = pl.pallas_call(
        fill_reply,
        out_shape=jax.ShapeDtypeStruct((far * TILE, dim), jnp.bfloat16),
        in_specs=[in_smem, in_vmem],
        out_specs=in_vmem,
        compiler_params=pltpu.CompilerParams(vmem_limit_bytes=SMALL_LIMIT),
        name="fill_reply",
    )(home, still)
    far_mine = lax.all_to_all(reply, "seq", split_axis=0, concat_axis=0, tiled=True)

    q2 = keep_in_hbm(queries.reshape(blocks * rows, dim))
    do2 = keep_in_hbm(d_out.reshape(blocks * rows, dim))
    blk = pl.BlockSpec((STEP * rows, dim), lambda b, *_: (b, 0))
    stat = pl.BlockSpec((STEP, 8, rows), lambda b, *_: (b, 0, 0))
    part_dq = pl.BlockSpec((STEP, dim, rows), lambda b, *_: (b, 0, 0))
    params = pltpu.CompilerParams(
        dimension_semantics=("arbitrary",), vmem_limit_bytes=VMEM_LIMIT
    )
    one = 2 * rows * TILE * dim
    bf16 = jnp.bfloat16
    own_rows, far_rows = (tok_rows, dim), (far * TILE, dim)
    some_keys = [pltpu.VMEM((2, WIDE * TILE, dim), bf16)] * 2
    some_probs = [pltpu.VMEM((2, WIDE * TILE, rows), bf16)] * 2

    stats = pl.pallas_call(
        functools.partial(own_stats, scale, heads),
        out_shape=jax.ShapeDtypeStruct((blocks, 8, rows), f32),
        grid_spec=pltpu.PrefetchScalarGridSpec(
            num_scalar_prefetch=2,
            grid=(blocks // STEP,),
            in_specs=[blk, blk, whole(own_rows), whole(own_rows)],
            out_specs=stat,
            scratch_shapes=[pltpu.VMEM((2,) + own_rows, bf16)] + some_keys + [pltpu.VMEM((STEP, 3, 8, rows), f32)],
        ),
        compiler_params=params,
        cost_estimate=pl.CostEstimate(
            flops=2 * one * blocks * 8, bytes_accessed=2 * tok_rows * heads * dim * 2, transcendentals=0
        ),
        name="own_stats",
    )(own_list, par, q2, do2, still, theirs)

    far_mine, stats = lax.optimization_barrier((far_mine, stats))
    far_theirs = swap_pair(far_mine)

    final, dq_part, far_keep, far_send = pl.pallas_call(
        functools.partial(far_grads, scale, inv_root),
        out_shape=(
            pltpu.HBM((blocks, 8, rows), f32),
            pltpu.HBM((blocks, dim, rows), f32),
            jax.ShapeDtypeStruct(far_rows, f32),
            jax.ShapeDtypeStruct(far_rows, bf16),
        ),
        grid_spec=pltpu.PrefetchScalarGridSpec(
            num_scalar_prefetch=2,
            grid=(blocks // STEP,),
            in_specs=[stat, blk, blk, whole(far_rows), whole(far_rows)],
            out_specs=(stat, part_dq, whole(far_rows), whole(far_rows)),
            scratch_shapes=[
                pltpu.VMEM((2,) + far_rows, bf16),
                pltpu.VMEM((2,) + far_rows, f32),
                pltpu.VMEM((STEP, WIDE * TILE, rows), f32),
                pltpu.VMEM((STEP, WIDE * TILE, rows), f32),
                pltpu.VMEM((STEP, 3, 8, rows), f32),
            ]
            + some_keys
            + some_probs,
        ),
        compiler_params=params,
        cost_estimate=pl.CostEstimate(
            flops=5 * one * blocks * 6, bytes_accessed=4 * tok_rows * heads * dim * 2, transcendentals=0
        ),
        name="far_grads",
    )(far_list, par, stats, q2, do2, far_mine, far_theirs)

    back = (far_keep + swap_pair(far_send).astype(f32)).astype(bf16)
    came = lax.all_to_all(back, "seq", split_axis=0, concat_axis=0, tiled=True)

    grad_q, own_keep, own_send = pl.pallas_call(
        functools.partial(own_grads, scale, inv_root, heads),
        out_shape=(
            jax.ShapeDtypeStruct((blocks * rows, dim), bf16),
            jax.ShapeDtypeStruct(own_rows, f32),
            jax.ShapeDtypeStruct(own_rows, f32),
        ),
        grid_spec=pltpu.PrefetchScalarGridSpec(
            num_scalar_prefetch=2,
            grid=(blocks // STEP,),
            in_specs=[stat, part_dq, blk, blk, whole(own_rows), whole(own_rows)],
            out_specs=(blk, whole(own_rows), whole(own_rows)),
            scratch_shapes=[
                pltpu.VMEM((2,) + own_rows, bf16),
                pltpu.VMEM((2,) + own_rows, f32),
                pltpu.VMEM((STEP, dim, rows), f32),
            ]
            + some_keys
            + some_probs,
        ),
        compiler_params=params,
        cost_estimate=pl.CostEstimate(
            flops=5 * one * blocks * 8, bytes_accessed=5 * tok_rows * heads * dim * 2, transcendentals=0
        ),
        name="own_grads",
    )(own_list, par, keep_in_hbm(final), keep_in_hbm(dq_part), q2, do2, still, theirs)

    other = swap_pair(own_send)
    grad_kv = pl.pallas_call(
        join_grads,
        out_shape=jax.ShapeDtypeStruct(own_rows, bf16),
        in_specs=[in_smem, in_vmem, in_vmem, in_vmem],
        out_specs=in_vmem,
        scratch_shapes=[pltpu.VMEM(own_rows, f32)],
        compiler_params=pltpu.CompilerParams(vmem_limit_bytes=SMALL_LIMIT),
        name="join_grads",
    )(home, own_keep, other, came)
    return (grad_q.reshape(tok_rows, heads, dim), grad_kv.reshape(tok_rows, 1, dim))


def solution(mesh):
    in_specs = (
        P("seq", "head", None),
        P("seq", "head", None),
        P("seq", None),
        P("seq", "head", None),
    )
    out_specs = (P("seq", "head", None), P("seq", "head", None))
    return jax.shard_map(
        on_device, mesh=mesh, in_specs=in_specs, out_specs=out_specs, check_vma=False
    )
```

```python
import functools
import math

import jax
import jax.numpy as jnp
from jax import lax
from jax.experimental import pallas as pl
from jax.experimental.pallas import tpu as pltpu
from jax.sharding import PartitionSpec as P

TILE = 64
SEL = 16
CAP = 3
WIDE = 8
OWN_SIZES = (2, 4, 5, 6, 7)
FAR_SIZES = (4, 7, 8)
VMEM_LIMIT = 40 * 1024 * 1024
SMALL_LIMIT = 8 * 1024 * 1024
OWN_GROUP, FAR_GROUP = 2, 4
STEP = 4
LOW = -1e30
HIGH = 1e30
TOO_LARGE = 2.0**64
NT = (((1,), (1,)), ((), ()))
TN = (((0,), (0,)), ((), ()))


def swap_pair(block):
    count = lax.axis_size("head")
    return lax.ppermute(block, "head", [(h, h ^ 1) for h in range(count)])


def keep_in_hbm(array):
    return pltpu.with_memory_space_constraint(array, pltpu.HBM)


def tile_rows(index):
    return pl.ds(pl.multiple_of(index * TILE, TILE), TILE)


def span(index, size):
    return pl.ds(pl.multiple_of(index * size, size), size)


def dot(a, b, dims=(((1,), (0,)), ((), ()))):
    return lax.dot_general(a, b, dims, preferred_element_type=jnp.float32)


def fold(x, op):
    parts = [x[8 * i : 8 * i + 8] for i in range(TILE // 8)]
    while len(parts) > 1:
        parts = [op(parts[i], parts[i + 1]) for i in range(0, len(parts), 2)]
    return parts[0]


def places(rows, group):
    key = lax.broadcasted_iota(jnp.int32, (TILE, rows), 0)
    query = lax.broadcasted_iota(jnp.int32, (TILE, rows), 1) // group
    return key, query


def mask_diagonal(x, is_first, group):
    key, query = places(x.shape[1], group)
    return jnp.where((key <= query) | jnp.logical_not(is_first), x, LOW)


def pick_diagonal(x, group):
    key, query = places(x.shape[1], group)
    return jnp.sum(fold(jnp.where(key == query, x, 0.0), jnp.add), axis=0, keepdims=True)


def lay_halves(par_ref, mine_ref, theirs_ref, kv_ref):
    par = par_ref[0]
    kv_ref[par] = mine_ref[...]
    kv_ref[1 - par] = theirs_ref[...]


def each_block(body):
    def run(j, _):
        body(pl.program_id(0) * STEP + j, j)
        return 0

    lax.fori_loop(0, STEP, run, 0)


def each_group(list_ref, size, body):
    def run(i, _):
        group = [(pl.program_id(0) * STEP + size * i + j, size * i + j) for j in range(size)]
        body(i, group, functools.reduce(jnp.maximum, [list_ref[b, SEL] for b, _ in group]))
        return 0

    lax.fori_loop(0, STEP // size, run, 0)


def pick(list_ref, b, start, size):
    count = list_ref[b, SEL]
    return (
        [list_ref[b, start + i] for i in range(size)],
        [start + i < count for i in range(size)],
    )


def part(i):
    return slice(i * TILE, (i + 1) * TILE)


def load_tiles(kv_ref, k_ref, v_ref, picks):
    for i, t in enumerate(picks):
        k_ref[part(i)] = kv_ref[0, tile_rows(t), :]
        v_ref[part(i)] = kv_ref[1, tile_rows(t), :]


def by_size(left, sizes, run):
    for low, size in zip((0,) + sizes[:-1], sizes, strict=True):

        @pl.when((left > low) & (left <= size))
        def _():
            run(size)


def in_parts(count, run):
    wide = count // WIDE

    def full(c, _):
        run(c * WIDE, WIDE)
        return 0

    lax.fori_loop(0, wide, full, 0)
    by_size(count - wide * WIDE, OWN_SIZES, lambda size: run(wide * WIDE, size))


def sum_up(x):
    return jnp.sum(x, axis=0, keepdims=True)


def own_stats(
    scale, group, list_ref, par_ref, q_ref, do_ref, mine_ref, theirs_ref, st_ref,
    kv_ref, k_ref, v_ref, sum_ref,
):
    rows = q_ref.shape[0] // STEP

    @pl.when(pl.program_id(0) == 0)
    def _():
        lay_halves(par_ref, mine_ref, theirs_ref, kv_ref)

    def scores(b, j, half, start, size):
        picks, real = pick(list_ref, b, start, size)
        load_tiles(kv_ref, k_ref.at[half], v_ref.at[half], picks)
        return dot(k_ref[half, : size * TILE], q_ref[span(j, rows), :], NT) * scale, real

    def run(b, j, half, start, size, fresh):
        x, real = scores(b, j, half, start, size)
        dp = dot(v_ref[half, : size * TILE], do_ref[span(j, rows), :], NT)
        base = sum_ref[j, 0]
        if fresh:
            base = jnp.where(start == 0, pick_diagonal(x[part(0)], group), base)
            sum_ref[j, 0] = base
        base = base[0:1]
        total, dotted = sum_ref[j, 1], sum_ref[j, 2]
        for i in range(size):
            xi = mask_diagonal(x[part(i)], start == 0, group) if i == 0 else x[part(i)]
            e = jnp.exp2(xi - jnp.where(real[i], base, HIGH))
            total = total + fold(e, jnp.add)
            dotted = dotted + fold(e * dp[part(i)], jnp.add)
        sum_ref[j, 1] = total
        sum_ref[j, 2] = dotted

    def first(_, pair, count):
        def both(start, size):
            for half, (b, j) in enumerate(pair):
                run(b, j, half, start, size, True)

        in_parts(count, both)

    def anew(b, j):
        count = list_ref[b, SEL]
        size = OWN_SIZES[0]
        clear = jnp.zeros(sum_ref.shape[2:], jnp.float32)
        sum_ref[j, 0] = clear + LOW

        def look(c, _):
            x, real = scores(b, j, 0, c * size, size)
            top = sum_ref[j, 0]
            for i in range(size):
                xi = mask_diagonal(x[part(i)], c == 0, group) if i == 0 else x[part(i)]
                top = jnp.maximum(top, jnp.where(real[i], fold(xi, jnp.maximum), LOW))
            sum_ref[j, 0] = top
            return 0

        def once_more(c, _):
            run(b, j, 0, c * size, size, False)
            return 0

        lax.fori_loop(0, pl.cdiv(count, size), look, 0)
        sum_ref[j, 0] = clear + jnp.max(sum_ref[j, 0], axis=0, keepdims=True)
        sum_ref[j, 1] = clear
        sum_ref[j, 2] = clear
        lax.fori_loop(0, pl.cdiv(count, size), once_more, 0)

    sum_ref[...] = jnp.zeros_like(sum_ref)
    each_group(list_ref, OWN_GROUP, first)

    @pl.when(jnp.max(sum_ref[:, 1]) > TOO_LARGE)
    def _():
        each_block(anew)

    for j in range(STEP):
        st_ref[j, 0:1] = sum_ref[j, 0, 0:1]
        st_ref[j, 1:2] = sum_up(sum_ref[j, 1])
        st_ref[j, 2:3] = sum_up(sum_ref[j, 2])


def add_grads(acc_ref, picks, gk, gv):
    for i, t in enumerate(picks):
        acc_ref[0, tile_rows(t), :] += gk[part(i)]
        acc_ref[1, tile_rows(t), :] += gv[part(i)]


def leave_grads(inv_root, par_ref, acc_ref, keep_ref, send_ref):
    @pl.when(pl.program_id(0) == pl.num_programs(0) - 1)
    def _():
        par = par_ref[0]
        keep = acc_ref[par] * jnp.where(par == 0, inv_root, 1.0)
        send = acc_ref[1 - par] * jnp.where(par == 0, 1.0, inv_root)
        keep_ref[...] = keep.astype(keep_ref.dtype)
        send_ref[...] = send.astype(send_ref.dtype)


def far_grads(
    scale, inv_root, list_ref, par_ref, st_ref, q_ref, do_ref, mine_ref, theirs_ref,
    fin_ref, dq_ref, keep_ref, send_ref,
    kv_ref, acc_ref, e_ref, dp_ref, sum_ref, k_ref, v_ref, p_ref, ds_ref,
):
    rows = q_ref.shape[0] // STEP

    @pl.when(pl.program_id(0) == 0)
    def _():
        lay_halves(par_ref, mine_ref, theirs_ref, kv_ref)
        acc_ref[...] = jnp.zeros_like(acc_ref)

    def begin(j, base):
        fade = jnp.exp2(st_ref[j, 0:1] - base)
        at_top = lax.broadcasted_iota(jnp.int32, sum_ref.shape[2:], 0) == 0
        sum_ref[j, 0] = jnp.broadcast_to(base, sum_ref.shape[2:])
        sum_ref[j, 1] = jnp.where(at_top, st_ref[j, 1:2] * fade, 0.0)
        sum_ref[j, 2] = jnp.where(at_top, st_ref[j, 2:3] * fade, 0.0)

    def scores(b, j, half, start, size):
        picks, real = pick(list_ref, b, start, size)
        load_tiles(kv_ref, k_ref.at[half], v_ref.at[half], picks)
        return dot(k_ref[half, : size * TILE], q_ref[span(j, rows), :], NT) * scale, real

    def read(b, j, half, start, size):
        x, real = scores(b, j, half, start, size)
        dp = dot(v_ref[half, : size * TILE], do_ref[span(j, rows), :], NT)
        base, total, dotted = sum_ref[j, 0, 0:1], sum_ref[j, 1], sum_ref[j, 2]
        for i in range(size):
            to = tile_rows(start + i)
            e = jnp.exp2(x[part(i)] - jnp.where(real[i], base, HIGH))
            e_ref[j, to, :] = e
            dp_ref[j, to, :] = dp[part(i)]
            total = total + fold(e, jnp.add)
            dotted = dotted + fold(e * dp[part(i)], jnp.add)
        sum_ref[j, 1] = total
        sum_ref[j, 2] = dotted

    def anew(b, j):
        count = list_ref[b, SEL]
        size = FAR_SIZES[0]
        sum_ref[j, 0] = jnp.broadcast_to(st_ref[j, 0:1], sum_ref.shape[2:])

        def look(c, _):
            x, real = scores(b, j, 0, c * size, size)
            top = sum_ref[j, 0]
            for i in range(size):
                top = jnp.maximum(top, jnp.where(real[i], fold(x[part(i)], jnp.maximum), LOW))
            sum_ref[j, 0] = top
            return 0

        def once_more(c, _):
            read(b, j, 0, c * size, size)
            return 0

        lax.fori_loop(0, pl.cdiv(count, size), look, 0)
        begin(j, jnp.max(sum_ref[j, 0], axis=0, keepdims=True))
        lax.fori_loop(0, pl.cdiv(count, size), once_more, 0)

    def finish(j):
        total, dotted = sum_up(sum_ref[j, 1]), sum_up(sum_ref[j, 2])
        delta = dotted / total
        fin_ref[j, 0:1] = sum_ref[j, 0, 0:1] + jnp.log2(total)
        fin_ref[j, 1:2] = delta
        fin_ref[j, 2:3] = 1.0 / total

    def spread(b, j, half, size):
        picks, _ = pick(list_ref, b, 0, size)
        delta, ratio = fin_ref[j, 1:2], fin_ref[j, 2:3]
        n = size * TILE
        q_at = span(j, rows)
        for i, t in enumerate(picks):
            k_ref[half, part(i)] = kv_ref[0, tile_rows(t), :]
            p = e_ref[j, part(i)] * ratio
            p_ref[half, part(i)] = p.astype(jnp.bfloat16)
            ds_ref[half, part(i)] = (p * (dp_ref[j, part(i)] - delta)).astype(jnp.bfloat16)
        ds = ds_ref[half, :n]
        add_grads(acc_ref, picks, dot(ds, q_ref[q_at, :]), dot(p_ref[half, :n], do_ref[q_at, :]))
        dq_ref[j] = dot(k_ref[half, :n], ds, TN)

    def first(_, pair, count):
        for _, j in pair:
            begin(j, st_ref[j, 0:1])

        def both(size):
            for half, (b, j) in enumerate(pair):
                read(b, j, half, 0, size)

        by_size(count, FAR_SIZES, both)

    def second(_, pair, count):
        for _, j in pair:
            finish(j)

        @pl.when(count == 0)
        def _():
            for _, j in pair:
                dq_ref[j] = jnp.zeros(dq_ref.shape[1:], dq_ref.dtype)

        def both(size):
            for half, (b, j) in enumerate(pair):
                spread(b, j, half, size)

        by_size(count, FAR_SIZES, both)

    each_group(list_ref, FAR_GROUP, first)

    @pl.when(jnp.max(sum_ref[:, 1]) > TOO_LARGE)
    def _():
        each_block(anew)

    each_group(list_ref, FAR_GROUP, second)
    leave_grads(inv_root, par_ref, acc_ref, keep_ref, send_ref)


def own_grads(
    scale, inv_root, group, list_ref, par_ref, fin_ref, part_ref, q_ref, do_ref, mine_ref, theirs_ref,
    out_ref, keep_ref, send_ref, kv_ref, acc_ref, dq_ref, k_ref, v_ref, p_ref, ds_ref,
):
    rows = q_ref.shape[0] // STEP

    @pl.when(pl.program_id(0) == 0)
    def _():
        lay_halves(par_ref, mine_ref, theirs_ref, kv_ref)
        acc_ref[...] = jnp.zeros_like(acc_ref)

    def write(j):
        out_ref[span(j, rows), :] = (dq_ref[j] * inv_root).astype(out_ref.dtype).T

    def spread(b, j, half, start, size):
        q_at = span(j, rows)
        picks, real = pick(list_ref, b, start, size)
        n = size * TILE
        load_tiles(kv_ref, k_ref.at[half], v_ref.at[half], picks)
        level = fin_ref[j, 0:1]
        delta = fin_ref[j, 1:2]
        x = dot(k_ref[half, :n], q_ref[q_at, :], NT) * scale
        dp = dot(v_ref[half, :n], do_ref[q_at, :], NT)
        for i in range(size):
            xi = mask_diagonal(x[part(i)], start == 0, group) if i == 0 else x[part(i)]
            p = jnp.exp2(xi - jnp.where(real[i], level, HIGH))
            p_ref[half, part(i)] = p.astype(jnp.bfloat16)
            ds_ref[half, part(i)] = (p * (dp[part(i)] - delta)).astype(jnp.bfloat16)
        ds = ds_ref[half, :n]
        add_grads(acc_ref, picks, dot(ds, q_ref[q_at, :]), dot(p_ref[half, :n], do_ref[q_at, :]))
        dq_ref[j] += dot(k_ref[half, :n], ds, TN)

    def work(i, pair, count):
        for _, j in pair:
            dq_ref[j] = part_ref[j]
        before = 2 * jnp.maximum(i - 1, 0)

        def both(start, size):
            for half, (b, j) in enumerate(pair):
                spread(b, j, half, start, size)
                write(before + half)

        in_parts(count, both)

    each_group(list_ref, OWN_GROUP, work)
    write(STEP - 2)
    write(STEP - 1)
    leave_grads(inv_root, par_ref, acc_ref, keep_ref, send_ref)


def fill_reply(home_ref, mine_ref, reply_ref):
    cap = home_ref.shape[2]
    for i in range(home_ref.shape[0] * cap):
        t = jnp.maximum(home_ref[i // cap, 0, i % cap], 0)
        reply_ref[i * TILE : (i + 1) * TILE] = mine_ref[tile_rows(t), :]


def join_grads(home_ref, keep_ref, other_ref, came_ref, out_ref, acc_ref):
    cap = home_ref.shape[2]
    acc_ref[...] = keep_ref[...] + other_ref[...]
    for i in range(home_ref.shape[0] * cap):
        t = home_ref[i // cap, 0, i % cap]

        @pl.when(t >= 0)
        def _():
            acc_ref[tile_rows(t), :] += came_ref[i * TILE : (i + 1) * TILE].astype(jnp.float32)

    out_ref[...] = acc_ref[...].astype(out_ref.dtype)


def plan(blocks, me_ref, sel_ref, ask_ref, own_ref, far_ref):
    shards = ask_ref.shape[0]
    tiles = shards * blocks
    f32, bf16 = jnp.float32, jnp.bfloat16
    me = me_ref[0]
    sel = sel_ref[...]
    rows = sel.shape[0]
    tile = lax.broadcasted_iota(jnp.int32, (rows, tiles), 1)
    named = sel[:, 0:1] == tile
    for s in range(1, SEL):
        named = named | (sel[:, s : s + 1] == tile)
    is_own = (tile // blocks == me) & (
        (me > 0) | (tile >= CAP) | (tile == lax.broadcasted_iota(jnp.int32, tile.shape, 0))
    )
    own = jnp.where(named & is_own, 1.0, 0.0)
    far = jnp.where(named & jnp.logical_not(is_own), 1.0, 0.0)
    wanted = jnp.max(far, axis=0, keepdims=True)

    a = lax.broadcasted_iota(jnp.int32, (tiles, tiles), 0)
    b = lax.broadcasted_iota(jnp.int32, (tiles, tiles), 1)
    lower = jnp.where(a < b, 1.0, 0.0).astype(bf16)
    higher = jnp.where(a > b, 1.0, 0.0).astype(bf16)
    same = jnp.where((a < b) & (a // blocks == b // blocks), 1.0, 0.0).astype(bf16)
    own_place = dot(own.astype(bf16), higher)
    far_place = dot(far.astype(bf16), lower)
    rank = dot(jnp.broadcast_to(wanted, (rows, tiles)).astype(bf16), same)

    local = (tile % blocks).astype(f32)
    far_index = (tile // blocks * CAP).astype(f32) + rank
    column = lax.broadcasted_iota(jnp.int32, (rows, 128), 1)

    def packed(flags, place, values, most):
        out = jnp.where(column == SEL, jnp.sum(flags, axis=1, keepdims=True), 0.0)
        for p in range(most):
            here = jnp.sum(jnp.where(place == p, flags * values, 0.0), axis=1, keepdims=True)
            out = jnp.where(column == p, here, out)
        return out.astype(jnp.int32)[:, : SEL + 1]

    own_ref[...] = packed(own, own_place, local, SEL)
    far_ref[...] = packed(far, far_place, far_index, FAR_SIZES[-1])

    spot = lax.broadcasted_iota(jnp.int32, (rows, tiles), 0).astype(f32)
    asked = jnp.where((rank == spot) & (wanted > 0.0), local + 1.0, 0.0).astype(bf16)
    shard = lax.broadcasted_iota(jnp.int32, (shards, tiles), 0)
    owned = lax.broadcasted_iota(jnp.int32, (shards, tiles), 1) // blocks == shard
    asked = dot(jnp.where(owned, 1.0, 0.0).astype(bf16), asked, NT).astype(jnp.int32) - 1
    for e in range(shards):
        ask_ref[e] = asked[e : e + 1, :CAP]


def whole(shape):
    return pl.BlockSpec(shape, lambda b, *_: (0,) * len(shape), pipeline_mode=pl.Buffered(1))


def on_device(queries, keyvals, selected, d_out):
    tok_rows, heads, dim = queries.shape
    blocks = tok_rows // TILE
    shards = lax.axis_size("seq")
    me = lax.axis_index("seq")
    par = (lax.axis_index("head") % 2).astype(jnp.int32).reshape(1)
    inv_root = dim**-0.5
    scale = inv_root / math.log(2.0)
    rows = TILE * heads
    far = shards * CAP
    f32 = jnp.float32

    mine = keyvals[:, 0, :]
    theirs = swap_pair(mine)
    still = keep_in_hbm(mine)

    in_smem = pl.BlockSpec(memory_space=pltpu.SMEM)
    in_vmem = pl.BlockSpec(memory_space=pltpu.VMEM)
    asked, own_list, far_list = pl.pallas_call(
        functools.partial(plan, blocks),
        out_shape=(
            jax.ShapeDtypeStruct((shards, 1, CAP), jnp.int32),
            jax.ShapeDtypeStruct((blocks, SEL + 1), jnp.int32),
            jax.ShapeDtypeStruct((blocks, SEL + 1), jnp.int32),
        ),
        in_specs=[in_smem, in_vmem],
        out_specs=(in_vmem, in_vmem, in_vmem),
        compiler_params=pltpu.CompilerParams(vmem_limit_bytes=SMALL_LIMIT),
        name="plan",
    )(me.astype(jnp.int32).reshape(1), keep_in_hbm(selected))
    home = lax.all_to_all(asked, "seq", split_axis=0, concat_axis=0, tiled=True)
    home, theirs = lax.optimization_barrier((home, theirs))
    theirs = keep_in_hbm(theirs)
    reply = pl.pallas_call(
        fill_reply,
        out_shape=jax.ShapeDtypeStruct((far * TILE, dim), jnp.bfloat16),
        in_specs=[in_smem, in_vmem],
        out_specs=in_vmem,
        compiler_params=pltpu.CompilerParams(vmem_limit_bytes=SMALL_LIMIT),
        name="fill_reply",
    )(home, still)
    far_mine = lax.all_to_all(reply, "seq", split_axis=0, concat_axis=0, tiled=True)

    q2 = keep_in_hbm(queries.reshape(blocks * rows, dim))
    do2 = keep_in_hbm(d_out.reshape(blocks * rows, dim))
    blk = pl.BlockSpec((STEP * rows, dim), lambda b, *_: (b, 0))
    stat = pl.BlockSpec((STEP, 8, rows), lambda b, *_: (b, 0, 0))
    part_dq = pl.BlockSpec((STEP, dim, rows), lambda b, *_: (b, 0, 0))
    params = pltpu.CompilerParams(
        dimension_semantics=("arbitrary",), vmem_limit_bytes=VMEM_LIMIT
    )
    one = 2 * rows * TILE * dim
    bf16 = jnp.bfloat16
    own_rows, far_rows = (tok_rows, dim), (far * TILE, dim)
    far_keys = [pltpu.VMEM((FAR_GROUP, WIDE * TILE, dim), bf16)] * 2
    far_probs = [pltpu.VMEM((FAR_GROUP, WIDE * TILE, rows), bf16)] * 2
    some_keys = [pltpu.VMEM((OWN_GROUP, WIDE * TILE, dim), bf16)] * 2
    some_probs = [pltpu.VMEM((OWN_GROUP, WIDE * TILE, rows), bf16)] * 2

    stats = pl.pallas_call(
        functools.partial(own_stats, scale, heads),
        out_shape=jax.ShapeDtypeStruct((blocks, 8, rows), f32),
        grid_spec=pltpu.PrefetchScalarGridSpec(
            num_scalar_prefetch=2,
            grid=(blocks // STEP,),
            in_specs=[blk, blk, whole(own_rows), whole(own_rows)],
            out_specs=stat,
            scratch_shapes=[pltpu.VMEM((2,) + own_rows, bf16)] + some_keys + [pltpu.VMEM((STEP, 3, 8, rows), f32)],
        ),
        compiler_params=params,
        cost_estimate=pl.CostEstimate(
            flops=2 * one * blocks * 8, bytes_accessed=2 * tok_rows * heads * dim * 2, transcendentals=0
        ),
        name="own_stats",
    )(own_list, par, q2, do2, still, theirs)

    far_mine, stats = lax.optimization_barrier((far_mine, stats))
    far_theirs = swap_pair(far_mine)

    final, dq_part, far_keep, far_send = pl.pallas_call(
        functools.partial(far_grads, scale, inv_root),
        out_shape=(
            pltpu.HBM((blocks, 8, rows), f32),
            pltpu.HBM((blocks, dim, rows), f32),
            jax.ShapeDtypeStruct(far_rows, f32),
            jax.ShapeDtypeStruct(far_rows, bf16),
        ),
        grid_spec=pltpu.PrefetchScalarGridSpec(
            num_scalar_prefetch=2,
            grid=(blocks // STEP,),
            in_specs=[stat, blk, blk, whole(far_rows), whole(far_rows)],
            out_specs=(stat, part_dq, whole(far_rows), whole(far_rows)),
            scratch_shapes=[
                pltpu.VMEM((2,) + far_rows, bf16),
                pltpu.VMEM((2,) + far_rows, f32),
                pltpu.VMEM((STEP, WIDE * TILE, rows), f32),
                pltpu.VMEM((STEP, WIDE * TILE, rows), f32),
                pltpu.VMEM((STEP, 3, 8, rows), f32),
            ]
            + far_keys
            + far_probs,
        ),
        compiler_params=params,
        cost_estimate=pl.CostEstimate(
            flops=5 * one * blocks * 6, bytes_accessed=4 * tok_rows * heads * dim * 2, transcendentals=0
        ),
        name="far_grads",
    )(far_list, par, stats, q2, do2, far_mine, far_theirs)

    back = (far_keep + swap_pair(far_send).astype(f32)).astype(bf16)
    came = lax.all_to_all(back, "seq", split_axis=0, concat_axis=0, tiled=True)

    grad_q, own_keep, own_send = pl.pallas_call(
        functools.partial(own_grads, scale, inv_root, heads),
        out_shape=(
            jax.ShapeDtypeStruct((blocks * rows, dim), bf16),
            jax.ShapeDtypeStruct(own_rows, f32),
            jax.ShapeDtypeStruct(own_rows, f32),
        ),
        grid_spec=pltpu.PrefetchScalarGridSpec(
            num_scalar_prefetch=2,
            grid=(blocks // STEP,),
            in_specs=[stat, part_dq, blk, blk, whole(own_rows), whole(own_rows)],
            out_specs=(blk, whole(own_rows), whole(own_rows)),
            scratch_shapes=[
                pltpu.VMEM((2,) + own_rows, bf16),
                pltpu.VMEM((2,) + own_rows, f32),
                pltpu.VMEM((STEP, dim, rows), f32),
            ]
            + some_keys
            + some_probs,
        ),
        compiler_params=params,
        cost_estimate=pl.CostEstimate(
            flops=5 * one * blocks * 8, bytes_accessed=5 * tok_rows * heads * dim * 2, transcendentals=0
        ),
        name="own_grads",
    )(own_list, par, keep_in_hbm(final), keep_in_hbm(dq_part), q2, do2, still, theirs)

    other = swap_pair(own_send)
    grad_kv = pl.pallas_call(
        join_grads,
        out_shape=jax.ShapeDtypeStruct(own_rows, bf16),
        in_specs=[in_smem, in_vmem, in_vmem, in_vmem],
        out_specs=in_vmem,
        scratch_shapes=[pltpu.VMEM(own_rows, f32)],
        compiler_params=pltpu.CompilerParams(vmem_limit_bytes=SMALL_LIMIT),
        name="join_grads",
    )(home, own_keep, other, came)
    return (grad_q.reshape(tok_rows, heads, dim), grad_kv.reshape(tok_rows, 1, dim))


def solution(mesh):
    in_specs = (
        P("seq", "head", None),
        P("seq", "head", None),
        P("seq", None),
        P("seq", "head", None),
    )
    out_specs = (P("seq", "head", None), P("seq", "head", None))
    return jax.shard_map(
        on_device, mesh=mesh, in_specs=in_specs, out_specs=out_specs, check_vma=False
    )
```

```python
import functools
import math

import jax
import jax.numpy as jnp
from jax import lax
from jax.experimental import pallas as pl
from jax.experimental.pallas import tpu as pltpu
from jax.sharding import PartitionSpec as P

TILE = 64
SEL = 16
CAP = 3
WIDE = 8
OWN_SIZES = (2, 4, 5, 6, 7)
FAR_SIZES = (4, 7, 8)
VMEM_LIMIT = 40 * 1024 * 1024
SMALL_LIMIT = 8 * 1024 * 1024
OWN_GROUP, FAR_GROUP = 2, 4
STEP = 4
LOW = -1e30
HIGH = 1e30
TOO_LARGE = 2.0**64
NT = (((1,), (1,)), ((), ()))
TN = (((0,), (0,)), ((), ()))


def swap_pair(block):
    count = lax.axis_size("head")
    return lax.ppermute(block, "head", [(h, h ^ 1) for h in range(count)])


def keep_in_hbm(array):
    return pltpu.with_memory_space_constraint(array, pltpu.HBM)


def tile_rows(index):
    return pl.ds(pl.multiple_of(index * TILE, TILE), TILE)


def span(index, size):
    return pl.ds(pl.multiple_of(index * size, size), size)


def dot(a, b, dims=(((1,), (0,)), ((), ()))):
    return lax.dot_general(a, b, dims, preferred_element_type=jnp.float32)


def fold(x, op):
    parts = [x[8 * i : 8 * i + 8] for i in range(TILE // 8)]
    while len(parts) > 1:
        parts = [op(parts[i], parts[i + 1]) for i in range(0, len(parts), 2)]
    return parts[0]


def places(rows, group):
    key = lax.broadcasted_iota(jnp.int32, (TILE, rows), 0)
    query = lax.broadcasted_iota(jnp.int32, (TILE, rows), 1) // group
    return key, query


def mask_diagonal(x, is_first, group):
    key, query = places(x.shape[1], group)
    return jnp.where((key <= query) | jnp.logical_not(is_first), x, LOW)


def pick_diagonal(x, group):
    key, query = places(x.shape[1], group)
    return jnp.sum(fold(jnp.where(key == query, x, 0.0), jnp.add), axis=0, keepdims=True)


def lay_halves(par_ref, mine_ref, theirs_ref, kv_ref):
    par = par_ref[0]
    kv_ref[par] = mine_ref[...]
    kv_ref[1 - par] = theirs_ref[...]


def each_block(body):
    def run(j, _):
        body(pl.program_id(0) * STEP + j, j)
        return 0

    lax.fori_loop(0, STEP, run, 0)


def each_group(list_ref, size, body):
    def run(i, _):
        group = [(pl.program_id(0) * STEP + size * i + j, size * i + j) for j in range(size)]
        body(i, group, functools.reduce(jnp.maximum, [list_ref[b, SEL] for b, _ in group]))
        return 0

    lax.fori_loop(0, STEP // size, run, 0)


def pick(list_ref, b, start, size):
    count = list_ref[b, SEL]
    return (
        [list_ref[b, start + i] for i in range(size)],
        [start + i < count for i in range(size)],
    )


def part(i):
    return slice(i * TILE, (i + 1) * TILE)


def load_tiles(kv_ref, k_ref, v_ref, picks):
    for i, t in enumerate(picks):
        k_ref[part(i)] = kv_ref[0, tile_rows(t), :]
        v_ref[part(i)] = kv_ref[1, tile_rows(t), :]


def by_size(left, sizes, run):
    for low, size in zip((0,) + sizes[:-1], sizes, strict=True):

        @pl.when((left > low) & (left <= size))
        def _():
            run(size)


def in_parts(count, run):
    wide = count // WIDE

    def full(c, _):
        run(c * WIDE, WIDE)
        return 0

    lax.fori_loop(0, wide, full, 0)
    by_size(count - wide * WIDE, OWN_SIZES, lambda size: run(wide * WIDE, size))


def sum_up(x):
    return jnp.sum(x, axis=0, keepdims=True)


def own_stats(
    scale, group, list_ref, par_ref, q_ref, do_ref, mine_ref, theirs_ref, st_ref,
    kv_ref, k_ref, v_ref, sum_ref,
):
    rows = q_ref.shape[0] // STEP

    @pl.when(pl.program_id(0) == 0)
    def _():
        lay_halves(par_ref, mine_ref, theirs_ref, kv_ref)

    def scores(b, j, half, start, size):
        picks, real = pick(list_ref, b, start, size)
        load_tiles(kv_ref, k_ref.at[half], v_ref.at[half], picks)
        return dot(k_ref[half, : size * TILE], q_ref[span(j, rows), :], NT) * scale, real

    def run(b, j, half, start, size, fresh):
        x, real = scores(b, j, half, start, size)
        dp = dot(v_ref[half, : size * TILE], do_ref[span(j, rows), :], NT)
        base = sum_ref[j, 0]
        if fresh:
            base = jnp.where(start == 0, pick_diagonal(x[part(0)], group), base)
            sum_ref[j, 0] = base
        base = base[0:1]
        total, dotted = sum_ref[j, 1], sum_ref[j, 2]
        for i in range(size):
            xi = mask_diagonal(x[part(i)], start == 0, group) if i == 0 else x[part(i)]
            e = jnp.exp2(xi - jnp.where(real[i], base, HIGH))
            total = total + fold(e, jnp.add)
            dotted = dotted + fold(e * dp[part(i)], jnp.add)
        sum_ref[j, 1] = total
        sum_ref[j, 2] = dotted

    def first(_, pair, count):
        def both(start, size):
            for half, (b, j) in enumerate(pair):
                run(b, j, half, start, size, True)

        in_parts(count, both)

    def anew(b, j):
        count = list_ref[b, SEL]
        size = OWN_SIZES[0]
        clear = jnp.zeros(sum_ref.shape[2:], jnp.float32)
        sum_ref[j, 0] = clear + LOW

        def look(c, _):
            x, real = scores(b, j, 0, c * size, size)
            top = sum_ref[j, 0]
            for i in range(size):
                xi = mask_diagonal(x[part(i)], c == 0, group) if i == 0 else x[part(i)]
                top = jnp.maximum(top, jnp.where(real[i], fold(xi, jnp.maximum), LOW))
            sum_ref[j, 0] = top
            return 0

        def once_more(c, _):
            run(b, j, 0, c * size, size, False)
            return 0

        lax.fori_loop(0, pl.cdiv(count, size), look, 0)
        sum_ref[j, 0] = clear + jnp.max(sum_ref[j, 0], axis=0, keepdims=True)
        sum_ref[j, 1] = clear
        sum_ref[j, 2] = clear
        lax.fori_loop(0, pl.cdiv(count, size), once_more, 0)

    sum_ref[...] = jnp.zeros_like(sum_ref)
    each_group(list_ref, OWN_GROUP, first)

    @pl.when(jnp.max(sum_ref[:, 1]) > TOO_LARGE)
    def _():
        each_block(anew)

    for j in range(STEP):
        st_ref[j, 0:1] = sum_ref[j, 0, 0:1]
        st_ref[j, 1:2] = sum_up(sum_ref[j, 1])
        st_ref[j, 2:3] = sum_up(sum_ref[j, 2])


def add_grads(acc_ref, picks, gk, gv):
    for i, t in enumerate(picks):
        acc_ref[0, tile_rows(t), :] += gk[part(i)]
        acc_ref[1, tile_rows(t), :] += gv[part(i)]


def leave_grads(inv_root, par_ref, acc_ref, keep_ref, send_ref):
    @pl.when(pl.program_id(0) == pl.num_programs(0) - 1)
    def _():
        par = par_ref[0]
        keep = acc_ref[par] * jnp.where(par == 0, inv_root, 1.0)
        send = acc_ref[1 - par] * jnp.where(par == 0, 1.0, inv_root)
        keep_ref[...] = keep.astype(keep_ref.dtype)
        send_ref[...] = send.astype(send_ref.dtype)


def far_grads(
    scale, inv_root, list_ref, par_ref, st_ref, q_ref, do_ref, mine_ref, theirs_ref,
    fin_ref, dq_ref, keep_ref, send_ref,
    kv_ref, acc_ref, e_ref, dp_ref, sum_ref, k_ref, v_ref, p_ref, ds_ref,
):
    rows = q_ref.shape[0] // STEP

    @pl.when(pl.program_id(0) == 0)
    def _():
        lay_halves(par_ref, mine_ref, theirs_ref, kv_ref)
        acc_ref[...] = jnp.zeros_like(acc_ref)

    def begin(j, base):
        fade = jnp.exp2(st_ref[j, 0:1] - base)
        at_top = lax.broadcasted_iota(jnp.int32, sum_ref.shape[2:], 0) == 0
        sum_ref[j, 0] = jnp.broadcast_to(base, sum_ref.shape[2:])
        sum_ref[j, 1] = jnp.where(at_top, st_ref[j, 1:2] * fade, 0.0)
        sum_ref[j, 2] = jnp.where(at_top, st_ref[j, 2:3] * fade, 0.0)

    def scores(b, j, half, start, size):
        picks, real = pick(list_ref, b, start, size)
        load_tiles(kv_ref, k_ref.at[half], v_ref.at[half], picks)
        return dot(k_ref[half, : size * TILE], q_ref[span(j, rows), :], NT) * scale, real

    def read(b, j, half, start, size):
        x, real = scores(b, j, half, start, size)
        dp = dot(v_ref[half, : size * TILE], do_ref[span(j, rows), :], NT)
        base, total, dotted = sum_ref[j, 0, 0:1], sum_ref[j, 1], sum_ref[j, 2]
        for i in range(size):
            to = tile_rows(start + i)
            e = jnp.exp2(x[part(i)] - jnp.where(real[i], base, HIGH))
            e_ref[j, to, :] = e
            dp_ref[j, to, :] = dp[part(i)]
            total = total + fold(e, jnp.add)
            dotted = dotted + fold(e * dp[part(i)], jnp.add)
        sum_ref[j, 1] = total
        sum_ref[j, 2] = dotted

    def anew(b, j):
        count = list_ref[b, SEL]
        size = FAR_SIZES[0]
        sum_ref[j, 0] = jnp.broadcast_to(st_ref[j, 0:1], sum_ref.shape[2:])

        def look(c, _):
            x, real = scores(b, j, 0, c * size, size)
            top = sum_ref[j, 0]
            for i in range(size):
                top = jnp.maximum(top, jnp.where(real[i], fold(x[part(i)], jnp.maximum), LOW))
            sum_ref[j, 0] = top
            return 0

        def once_more(c, _):
            read(b, j, 0, c * size, size)
            return 0

        lax.fori_loop(0, pl.cdiv(count, size), look, 0)
        begin(j, jnp.max(sum_ref[j, 0], axis=0, keepdims=True))
        lax.fori_loop(0, pl.cdiv(count, size), once_more, 0)

    def finish(j):
        total, dotted = sum_up(sum_ref[j, 1]), sum_up(sum_ref[j, 2])
        delta = dotted / total
        fin_ref[j, 0:1] = sum_ref[j, 0, 0:1] + jnp.log2(total)
        fin_ref[j, 1:2] = delta
        fin_ref[j, 2:3] = 1.0 / total

    def spread(b, j, half, size):
        picks, _ = pick(list_ref, b, 0, size)
        delta, ratio = fin_ref[j, 1:2], fin_ref[j, 2:3]
        n = size * TILE
        q_at = span(j, rows)
        for i, t in enumerate(picks):
            k_ref[half, part(i)] = kv_ref[0, tile_rows(t), :]
            p = e_ref[j, part(i)] * ratio
            p_ref[half, part(i)] = p.astype(jnp.bfloat16)
            ds_ref[half, part(i)] = (p * (dp_ref[j, part(i)] - delta)).astype(jnp.bfloat16)
        ds = ds_ref[half, :n]
        add_grads(acc_ref, picks, dot(ds, q_ref[q_at, :]), dot(p_ref[half, :n], do_ref[q_at, :]))
        dq_ref[j] = dot(k_ref[half, :n], ds, TN)

    def first(_, pair, count):
        for _, j in pair:
            begin(j, st_ref[j, 0:1])

        def both(size):
            for half, (b, j) in enumerate(pair):
                read(b, j, half, 0, size)

        by_size(count, FAR_SIZES, both)

    def second(_, pair, count):
        for _, j in pair:
            finish(j)

        @pl.when(count == 0)
        def _():
            for _, j in pair:
                dq_ref[j] = jnp.zeros(dq_ref.shape[1:], dq_ref.dtype)

        def both(size):
            for half, (b, j) in enumerate(pair):
                spread(b, j, half, size)

        by_size(count, FAR_SIZES, both)

    each_group(list_ref, FAR_GROUP, first)

    @pl.when(jnp.max(sum_ref[:, 1]) > TOO_LARGE)
    def _():
        each_block(anew)

    each_group(list_ref, FAR_GROUP, second)
    leave_grads(inv_root, par_ref, acc_ref, keep_ref, send_ref)


def own_grads(
    scale, inv_root, group, list_ref, par_ref, fin_ref, part_ref, q_ref, do_ref, mine_ref, theirs_ref,
    out_ref, keep_ref, send_ref, kv_ref, acc_ref, dq_ref, k_ref, v_ref, p_ref, ds_ref,
):
    rows = q_ref.shape[0] // STEP

    @pl.when(pl.program_id(0) == 0)
    def _():
        lay_halves(par_ref, mine_ref, theirs_ref, kv_ref)
        acc_ref[...] = jnp.zeros_like(acc_ref)

    def write(j):
        out_ref[span(j, rows), :] = (dq_ref[j] * inv_root).astype(out_ref.dtype).T

    def spread(b, j, half, start, size):
        q_at = span(j, rows)
        picks, real = pick(list_ref, b, start, size)
        n = size * TILE
        load_tiles(kv_ref, k_ref.at[half], v_ref.at[half], picks)
        level = fin_ref[j, 0:1]
        delta = fin_ref[j, 1:2]
        x = dot(k_ref[half, :n], q_ref[q_at, :], NT) * scale
        dp = dot(v_ref[half, :n], do_ref[q_at, :], NT)
        for i in range(size):
            xi = mask_diagonal(x[part(i)], start == 0, group) if i == 0 else x[part(i)]
            p = jnp.exp2(xi - jnp.where(real[i], level, HIGH))
            p_ref[half, part(i)] = p.astype(jnp.bfloat16)
            ds_ref[half, part(i)] = (p * (dp[part(i)] - delta)).astype(jnp.bfloat16)

    def gather(b, j, half, start, size):
        q_at = span(j, rows)
        picks, _ = pick(list_ref, b, start, size)
        n = size * TILE
        ds = ds_ref[half, :n]
        add_grads(acc_ref, picks, dot(ds, q_ref[q_at, :]), dot(p_ref[half, :n], do_ref[q_at, :]))
        dq_ref[j] += dot(k_ref[half, :n], ds, TN)

    def work(i, pair, count):
        for _, j in pair:
            dq_ref[j] = part_ref[j]
        before = 2 * jnp.maximum(i - 1, 0)

        def both(start, size):
            for half, (b, j) in enumerate(pair):
                spread(b, j, half, start, size)
            for half, (b, j) in enumerate(pair):
                gather(b, j, half, start, size)
                write(before + half)

        in_parts(count, both)

    each_group(list_ref, OWN_GROUP, work)
    write(STEP - 2)
    write(STEP - 1)
    leave_grads(inv_root, par_ref, acc_ref, keep_ref, send_ref)


def fill_reply(home_ref, mine_ref, reply_ref):
    cap = home_ref.shape[2]
    for i in range(home_ref.shape[0] * cap):
        t = jnp.maximum(home_ref[i // cap, 0, i % cap], 0)
        reply_ref[i * TILE : (i + 1) * TILE] = mine_ref[tile_rows(t), :]


def join_grads(home_ref, keep_ref, other_ref, came_ref, out_ref, acc_ref):
    cap = home_ref.shape[2]
    acc_ref[...] = keep_ref[...] + other_ref[...]
    for i in range(home_ref.shape[0] * cap):
        t = home_ref[i // cap, 0, i % cap]

        @pl.when(t >= 0)
        def _():
            acc_ref[tile_rows(t), :] += came_ref[i * TILE : (i + 1) * TILE].astype(jnp.float32)

    out_ref[...] = acc_ref[...].astype(out_ref.dtype)


def plan(blocks, me_ref, sel_ref, ask_ref, own_ref, far_ref):
    shards = ask_ref.shape[0]
    tiles = shards * blocks
    f32, bf16 = jnp.float32, jnp.bfloat16
    me = me_ref[0]
    sel = sel_ref[...]
    rows = sel.shape[0]
    tile = lax.broadcasted_iota(jnp.int32, (rows, tiles), 1)
    named = sel[:, 0:1] == tile
    for s in range(1, SEL):
        named = named | (sel[:, s : s + 1] == tile)
    is_own = (tile // blocks == me) & (
        (me > 0) | (tile >= CAP) | (tile == lax.broadcasted_iota(jnp.int32, tile.shape, 0))
    )
    own = jnp.where(named & is_own, 1.0, 0.0)
    far = jnp.where(named & jnp.logical_not(is_own), 1.0, 0.0)
    wanted = jnp.max(far, axis=0, keepdims=True)

    a = lax.broadcasted_iota(jnp.int32, (tiles, tiles), 0)
    b = lax.broadcasted_iota(jnp.int32, (tiles, tiles), 1)
    lower = jnp.where(a < b, 1.0, 0.0).astype(bf16)
    higher = jnp.where(a > b, 1.0, 0.0).astype(bf16)
    same = jnp.where((a < b) & (a // blocks == b // blocks), 1.0, 0.0).astype(bf16)
    own_place = dot(own.astype(bf16), higher)
    far_place = dot(far.astype(bf16), lower)
    rank = dot(jnp.broadcast_to(wanted, (rows, tiles)).astype(bf16), same)

    local = (tile % blocks).astype(f32)
    far_index = (tile // blocks * CAP).astype(f32) + rank
    column = lax.broadcasted_iota(jnp.int32, (rows, 128), 1)

    def packed(flags, place, values, most):
        out = jnp.where(column == SEL, jnp.sum(flags, axis=1, keepdims=True), 0.0)
        for p in range(most):
            here = jnp.sum(jnp.where(place == p, flags * values, 0.0), axis=1, keepdims=True)
            out = jnp.where(column == p, here, out)
        return out.astype(jnp.int32)[:, : SEL + 1]

    own_ref[...] = packed(own, own_place, local, SEL)
    far_ref[...] = packed(far, far_place, far_index, FAR_SIZES[-1])

    spot = lax.broadcasted_iota(jnp.int32, (rows, tiles), 0).astype(f32)
    asked = jnp.where((rank == spot) & (wanted > 0.0), local + 1.0, 0.0).astype(bf16)
    shard = lax.broadcasted_iota(jnp.int32, (shards, tiles), 0)
    owned = lax.broadcasted_iota(jnp.int32, (shards, tiles), 1) // blocks == shard
    asked = dot(jnp.where(owned, 1.0, 0.0).astype(bf16), asked, NT).astype(jnp.int32) - 1
    for e in range(shards):
        ask_ref[e] = asked[e : e + 1, :CAP]


def whole(shape):
    return pl.BlockSpec(shape, lambda b, *_: (0,) * len(shape), pipeline_mode=pl.Buffered(1))


def on_device(queries, keyvals, selected, d_out):
    tok_rows, heads, dim = queries.shape
    blocks = tok_rows // TILE
    shards = lax.axis_size("seq")
    me = lax.axis_index("seq")
    par = (lax.axis_index("head") % 2).astype(jnp.int32).reshape(1)
    inv_root = dim**-0.5
    scale = inv_root / math.log(2.0)
    rows = TILE * heads
    far = shards * CAP
    f32 = jnp.float32

    mine = keyvals[:, 0, :]
    theirs = swap_pair(mine)
    still = keep_in_hbm(mine)

    in_smem = pl.BlockSpec(memory_space=pltpu.SMEM)
    in_vmem = pl.BlockSpec(memory_space=pltpu.VMEM)
    asked, own_list, far_list = pl.pallas_call(
        functools.partial(plan, blocks),
        out_shape=(
            jax.ShapeDtypeStruct((shards, 1, CAP), jnp.int32),
            jax.ShapeDtypeStruct((blocks, SEL + 1), jnp.int32),
            jax.ShapeDtypeStruct((blocks, SEL + 1), jnp.int32),
        ),
        in_specs=[in_smem, in_vmem],
        out_specs=(in_vmem, in_vmem, in_vmem),
        compiler_params=pltpu.CompilerParams(vmem_limit_bytes=SMALL_LIMIT),
        name="plan",
    )(me.astype(jnp.int32).reshape(1), keep_in_hbm(selected))
    home = lax.all_to_all(asked, "seq", split_axis=0, concat_axis=0, tiled=True)
    home, theirs = lax.optimization_barrier((home, theirs))
    theirs = keep_in_hbm(theirs)
    reply = pl.pallas_call(
        fill_reply,
        out_shape=jax.ShapeDtypeStruct((far * TILE, dim), jnp.bfloat16),
        in_specs=[in_smem, in_vmem],
        out_specs=in_vmem,
        compiler_params=pltpu.CompilerParams(vmem_limit_bytes=SMALL_LIMIT),
        name="fill_reply",
    )(home, still)
    far_mine = lax.all_to_all(reply, "seq", split_axis=0, concat_axis=0, tiled=True)

    q2 = keep_in_hbm(queries.reshape(blocks * rows, dim))
    do2 = keep_in_hbm(d_out.reshape(blocks * rows, dim))
    blk = pl.BlockSpec((STEP * rows, dim), lambda b, *_: (b, 0))
    stat = pl.BlockSpec((STEP, 8, rows), lambda b, *_: (b, 0, 0))
    part_dq = pl.BlockSpec((STEP, dim, rows), lambda b, *_: (b, 0, 0))
    params = pltpu.CompilerParams(
        dimension_semantics=("arbitrary",), vmem_limit_bytes=VMEM_LIMIT
    )
    one = 2 * rows * TILE * dim
    bf16 = jnp.bfloat16
    own_rows, far_rows = (tok_rows, dim), (far * TILE, dim)
    far_keys = [pltpu.VMEM((FAR_GROUP, WIDE * TILE, dim), bf16)] * 2
    far_probs = [pltpu.VMEM((FAR_GROUP, WIDE * TILE, rows), bf16)] * 2
    some_keys = [pltpu.VMEM((OWN_GROUP, WIDE * TILE, dim), bf16)] * 2
    some_probs = [pltpu.VMEM((OWN_GROUP, WIDE * TILE, rows), bf16)] * 2

    stats = pl.pallas_call(
        functools.partial(own_stats, scale, heads),
        out_shape=jax.ShapeDtypeStruct((blocks, 8, rows), f32),
        grid_spec=pltpu.PrefetchScalarGridSpec(
            num_scalar_prefetch=2,
            grid=(blocks // STEP,),
            in_specs=[blk, blk, whole(own_rows), whole(own_rows)],
            out_specs=stat,
            scratch_shapes=[pltpu.VMEM((2,) + own_rows, bf16)] + some_keys + [pltpu.VMEM((STEP, 3, 8, rows), f32)],
        ),
        compiler_params=params,
        cost_estimate=pl.CostEstimate(
            flops=2 * one * blocks * 8, bytes_accessed=2 * tok_rows * heads * dim * 2, transcendentals=0
        ),
        name="own_stats",
    )(own_list, par, q2, do2, still, theirs)

    far_mine, stats = lax.optimization_barrier((far_mine, stats))
    far_theirs = swap_pair(far_mine)

    final, dq_part, far_keep, far_send = pl.pallas_call(
        functools.partial(far_grads, scale, inv_root),
        out_shape=(
            pltpu.HBM((blocks, 8, rows), f32),
            pltpu.HBM((blocks, dim, rows), f32),
            jax.ShapeDtypeStruct(far_rows, f32),
            jax.ShapeDtypeStruct(far_rows, bf16),
        ),
        grid_spec=pltpu.PrefetchScalarGridSpec(
            num_scalar_prefetch=2,
            grid=(blocks // STEP,),
            in_specs=[stat, blk, blk, whole(far_rows), whole(far_rows)],
            out_specs=(stat, part_dq, whole(far_rows), whole(far_rows)),
            scratch_shapes=[
                pltpu.VMEM((2,) + far_rows, bf16),
                pltpu.VMEM((2,) + far_rows, f32),
                pltpu.VMEM((STEP, WIDE * TILE, rows), f32),
                pltpu.VMEM((STEP, WIDE * TILE, rows), f32),
                pltpu.VMEM((STEP, 3, 8, rows), f32),
            ]
            + far_keys
            + far_probs,
        ),
        compiler_params=params,
        cost_estimate=pl.CostEstimate(
            flops=5 * one * blocks * 6, bytes_accessed=4 * tok_rows * heads * dim * 2, transcendentals=0
        ),
        name="far_grads",
    )(far_list, par, stats, q2, do2, far_mine, far_theirs)

    back = (far_keep + swap_pair(far_send).astype(f32)).astype(bf16)
    came = lax.all_to_all(back, "seq", split_axis=0, concat_axis=0, tiled=True)

    grad_q, own_keep, own_send = pl.pallas_call(
        functools.partial(own_grads, scale, inv_root, heads),
        out_shape=(
            jax.ShapeDtypeStruct((blocks * rows, dim), bf16),
            jax.ShapeDtypeStruct(own_rows, f32),
            jax.ShapeDtypeStruct(own_rows, f32),
        ),
        grid_spec=pltpu.PrefetchScalarGridSpec(
            num_scalar_prefetch=2,
            grid=(blocks // STEP,),
            in_specs=[stat, part_dq, blk, blk, whole(own_rows), whole(own_rows)],
            out_specs=(blk, whole(own_rows), whole(own_rows)),
            scratch_shapes=[
                pltpu.VMEM((2,) + own_rows, bf16),
                pltpu.VMEM((2,) + own_rows, f32),
                pltpu.VMEM((STEP, dim, rows), f32),
            ]
            + some_keys
            + some_probs,
        ),
        compiler_params=params,
        cost_estimate=pl.CostEstimate(
            flops=5 * one * blocks * 8, bytes_accessed=5 * tok_rows * heads * dim * 2, transcendentals=0
        ),
        name="own_grads",
    )(own_list, par, keep_in_hbm(final), keep_in_hbm(dq_part), q2, do2, still, theirs)

    other = swap_pair(own_send)
    grad_kv = pl.pallas_call(
        join_grads,
        out_shape=jax.ShapeDtypeStruct(own_rows, bf16),
        in_specs=[in_smem, in_vmem, in_vmem, in_vmem],
        out_specs=in_vmem,
        scratch_shapes=[pltpu.VMEM(own_rows, f32)],
        compiler_params=pltpu.CompilerParams(vmem_limit_bytes=SMALL_LIMIT),
        name="join_grads",
    )(home, own_keep, other, came)
    return (grad_q.reshape(tok_rows, heads, dim), grad_kv.reshape(tok_rows, 1, dim))


def solution(mesh):
    in_specs = (
        P("seq", "head", None),
        P("seq", "head", None),
        P("seq", None),
        P("seq", "head", None),
    )
    out_specs = (P("seq", "head", None), P("seq", "head", None))
    return jax.shard_map(
        on_device, mesh=mesh, in_specs=in_specs, out_specs=out_specs, check_vma=False
    )
```
